32 devices in a mesh: fsdp: 8 (over y, x, core), tensor: 4 (over z).
Axes of the slice: x: 2, y: 2, z: 4, core: 2. Of those that a mesh axis runs over, the one named last changes fastest.
Arguments:
- tokens: bfloat16 [24, 729, 1152], P('fsdp'), may hold values from -6 to 6
- slot_valid: int32 [24], P('fsdp'), may hold values 0 or 1
- ln1_gain: bfloat16 [1152], P('tensor'), may hold values from 0.5 to 1.5
- ln1_bias: bfloat16 [1152], P('tensor'), may hold values from -1.5 to 1.5
- w_qkv: bfloat16 [3, 1152, 1152], P(None, 'fsdp', 'tensor'), may hold values from -0.1875 to 0.1875
- b_query: bfloat16 [1152], P('tensor'), may hold values from -1.5 to 1.5
- b_value: bfloat16 [1152], P('tensor'), may hold values from -0.25 to 0.25
- w_out: bfloat16 [1152, 1152], P('tensor', 'fsdp'), may hold values from -3 to 3
- b_out: bfloat16 [1152], P('tensor'), may hold values from -1.5 to 1.5
- ln2_gain: bfloat16 [1152], P('tensor'), may hold values from 0.5 to 1.5
- ln2_bias: bfloat16 [1152], P('tensor'), may hold values from -1.5 to 1.5
- w_up: bfloat16 [1152, 4304], P('fsdp', 'tensor'), may hold values from -0.1875 to 0.1875
- b_up: bfloat16 [4304], P('tensor'), may hold values from -1.5 to 1.5
- w_down: bfloat16 [4304, 1152], P('tensor', 'fsdp'), may hold values from -0.09375 to 0.09375
- b_down: bfloat16 [1152], P('tensor'), may hold values from -1.5 to 1.5
- grad_out: bfloat16 [24, 729, 1152], P('fsdp'), may hold values from -6 to 6
Outputs:
- layer_out: bfloat16 [24, 729, 1152], P('fsdp')
- grad_tokens: float32 [24, 729, 1152], P('fsdp')
- grad_ln1_gain: float32 [1152], P('tensor')
- grad_ln1_bias: float32 [1152], P('tensor')
- grad_qkv: float32 [3, 1152, 1152], P(None, 'fsdp', 'tensor')
- grad_b_query: float32 [1152], P('tensor')
- grad_b_value: float32 [1152], P('tensor')
- grad_w_out: float32 [1152, 1152], P('tensor', 'fsdp')
- grad_b_out: float32 [1152], P('tensor')
- grad_ln2_gain: float32 [1152], P('tensor')
- grad_ln2_bias: float32 [1152], P('tensor')
- grad_w_up: float32 [1152, 4304], P('fsdp', 'tensor')
- grad_b_up: float32 [4304], P('tensor')
- grad_w_down: float32 [4304, 1152], P('tensor', 'fsdp')
- grad_b_down: float32 [1152], P('tensor')
- head_max: float32 [16], P('tensor')
- clipped_qk: float32 [2, 1152, 1152], P(None, 'fsdp', 'tensor')
- clipped_b_query: float32 [1152], P('tensor')
The draws below stay inside these ranges and needn't reach their ends.
Inputs may be any that keep to these rules, and one draw needn't show every extreme that they name: `slot_valid`: 1 marks a slot that holds an image, 0 an empty slot.
All inputs are finite; a program needn't handle non-finite values. No bound on the sum of `slot_valid` on one device may be relied on, other than what follows from the above.
Results may differ from the reference program's by a relative error of at most 0.02.
Values may be sent and summed in bfloat16 or wider, within the bound.
A program may use at most 192 MiB of HBM per device.

```python
import jax
import jax.numpy as jnp
from jax import lax

D = 1152
HEADS = 16
HD = 72
FF = 4304
SEQ = 729
CLIP = 4
INNER = 1152
SLOTS = 24


def touch_ends(drawn, own_key, low, top_value):
    shape = drawn.shape
    place = [jax.random.randint(jax.random.fold_in(own_key, axis), (), 0, shape[axis]) for axis in range(len(shape))]
    drawn = drawn.at[tuple(place)].set(low)
    longest = shape.index(max(shape))
    place[longest] = (place[longest] + 1) % shape[longest]
    return drawn.at[tuple(place)].set(top_value)


def steps_of(own_key, extent, split, smallest, largest):
    factor_of, own = 1.0, jax.random.fold_in(own_key, 6)
    for dim, shards_of in split:
        steps = jnp.exp(jax.random.uniform(jax.random.fold_in(own, dim), (shards_of,), jnp.float32, smallest / len(split), largest / len(split)))
        factor_of = factor_of * jnp.repeat(steps, extent[dim] // shards_of).reshape([-1 if axis == dim else 1 for axis in range(len(extent))])
    return factor_of


def scatter_about(stream_key, shape, width, limit, pieces=(), kind=jnp.bfloat16):
    gain = steps_of(stream_key, shape, pieces, -0.22, 0.18) if pieces else 1.0
    values = jax.random.normal(stream_key, shape, jnp.float32) * width * gain
    return jnp.minimum(jnp.maximum(values, -limit), limit).astype(kind)


def setup_inputs(seed: int = 0) -> dict:
    streams_of = jax.random.split(jax.random.key(seed), 17)
    tokens = scatter_about(streams_of[0], (SLOTS, SEQ, D), 1.0, 6.0, ((0, 8),))
    slot_valid = touch_ends((jax.random.randint(streams_of[1], (SLOTS,), 0, 16) < 15).astype(jnp.int32), jax.random.fold_in(streams_of[1], 1), 0, 1)
    ln1_gain = jnp.clip(1.0 + 0.1 * jax.random.normal(streams_of[2], (D,), jnp.float32), 0.5, 1.5).astype(jnp.bfloat16)
    ln1_bias = scatter_about(streams_of[3], (D,), 0.3, 1.5, ((0, 4),))
    w_qkv = scatter_about(streams_of[4], (3, D, INNER), D ** -0.5, 0.1875, ((1, 8), (2, 4)))
    b_query = scatter_about(streams_of[5], (INNER,), 0.3, 1.5, ((0, 4),))
    b_value = scatter_about(streams_of[6], (INNER,), 0.05, 0.25, ((0, 4),))
    w_out = scatter_about(streams_of[7], (INNER, D), 4 ** -0.5, 3.0, ((0, 4), (1, 8)))
    b_out = scatter_about(streams_of[8], (D,), 0.3, 1.5, ((0, 4),))
    ln2_gain = jnp.clip(1.0 + 0.1 * jax.random.normal(streams_of[9], (D,), jnp.float32), 0.5, 1.5).astype(jnp.bfloat16)
    ln2_bias = scatter_about(streams_of[10], (D,), 0.3, 1.5, ((0, 4),))
    w_up = scatter_about(streams_of[11], (D, FF), D ** -0.5, 0.1875, ((0, 8), (1, 4)))
    b_up = scatter_about(streams_of[12], (FF,), 0.3, 1.5, ((0, 4),))
    w_down = scatter_about(streams_of[13], (FF, D), FF ** -0.5, 0.09375, ((0, 4), (1, 8)))
    b_down = scatter_about(streams_of[14], (D,), 0.3, 1.5, ((0, 4),))
    grad_out = scatter_about(streams_of[15], (SLOTS, SEQ, D), 1.0, 6.0, ((0, 8),))
    return dict(tokens=tokens, slot_valid=slot_valid, ln1_gain=ln1_gain, ln1_bias=ln1_bias, w_qkv=w_qkv, b_query=b_query, b_value=b_value, w_out=w_out, b_out=b_out, ln2_gain=ln2_gain, ln2_bias=ln2_bias, w_up=w_up, b_up=b_up, w_down=w_down, b_down=b_down, grad_out=grad_out)


epsilon = 1e-06
highest = lax.Precision.HIGHEST

@jax.custom_vjp
def low(v):
    return lax.optimization_barrier(v.astype(jnp.bfloat16)).astype(jnp.float32)

@jax.custom_vjp
def low_back(v):
    return v

def low_keep(v):
    return (low(v), None)

def low_pass(kept, grad):
    return (grad,)

def back_keep(v):
    return (v, None)

def back_low(kept, grad):
    return (low(grad),)
low.defvjp(low_keep, low_pass)
low_back.defvjp(back_keep, back_low)

def matmul(left, right):
    return jnp.dot(left, right, precision=highest, preferred_element_type=jnp.float32)

def norm_rows(row_block, gain_vec, shift_vec):
    centre = lax.optimization_barrier(jnp.mean(row_block, axis=-1, keepdims=True))
    centred = row_block - centre
    spread = lax.optimization_barrier(jnp.mean(centred * centred, axis=-1, keepdims=True))
    return centred * lax.rsqrt(spread + epsilon) * gain_vec + shift_vec

def one_image(image_rows, params):
    gain_one, bias_one, qkv_weight, query_bias, value_bias, out_weight, out_bias, gain_two, bias_two, up_weight, up_bias, down_weight, down_bias = params
    normed_one = low(norm_rows(image_rows, gain_one, bias_one))
    query_rows = low(low_back(matmul(normed_one, qkv_weight[0]) + query_bias)).reshape(SEQ, HEADS, HD)
    key_rows = low(low_back(matmul(normed_one, qkv_weight[1]))).reshape(SEQ, HEADS, HD)
    value_rows = low(low_back(matmul(normed_one, qkv_weight[2]) + value_bias)).reshape(SEQ, HEADS, HD)
    raw_scores = low_back(jnp.einsum('qhd,khd->hqk', query_rows, key_rows, precision=highest))
    scores = raw_scores * HD ** (-0.5)
    head_peak = lax.optimization_barrier(jnp.max(scores, axis=(1, 2)))
    attn_probs = jax.nn.softmax(scores, axis=-1)
    mixed_rows = jnp.einsum('hqk,khd->qhd', low(attn_probs), value_rows, precision=highest)
    heads_out = low(low_back(mixed_rows.reshape(SEQ, INNER)))
    attn_rows = low_back(matmul(heads_out, out_weight) + out_bias)
    residual = image_rows + attn_rows
    normed_two = low(norm_rows(residual, gain_two, bias_two))
    pre_act = low_back(matmul(normed_two, up_weight) + up_bias)
    activated = low(jax.nn.gelu(pre_act, approximate=True))
    return (residual + matmul(activated, down_weight) + down_bias, head_peak)

def reference(tokens, slot_valid, ln1_gain, ln1_bias, w_qkv, b_query, b_value, w_out, b_out, ln2_gain, ln2_bias, w_up, b_up, w_down, b_down, grad_out):
    params = tuple((weight.astype(jnp.float32) for weight in (ln1_gain, ln1_bias, w_qkv, b_query, b_value, w_out, b_out, ln2_gain, ln2_bias, w_up, b_up, w_down, b_down)))
    keep_mask = slot_valid.astype(jnp.float32)[:, None, None]

    def forward(image_block, weights):

        def per_image(image_rows):
            return one_image(image_rows, weights)
        layer_rows, peaks = lax.map(jax.checkpoint(per_image), image_block)
        return (layer_rows * keep_mask, peaks)
    layer_rows, pull_back, peaks = jax.vjp(forward, tokens.astype(jnp.float32), params, has_aux=True)
    grad_rows, grads = pull_back(grad_out.astype(jnp.float32))
    head_peak = lax.optimization_barrier(jnp.max(jnp.where((slot_valid > 0)[:, None], peaks, -1e+30), axis=0))
    factor = jnp.repeat(jnp.sqrt(CLIP / jnp.maximum(head_peak, CLIP * 1.0)), HD)
    qkv_weight = params[2]
    clipped = jnp.stack([qkv_weight[0] * factor, qkv_weight[1] * factor])
    return (layer_rows.astype(jnp.bfloat16), grad_rows, grads[0], grads[1], grads[2], grads[3], grads[4], grads[5], grads[6], grads[7], grads[8], grads[9], grads[10], grads[11], grads[12], head_peak, clipped, params[3] * factor)
```

```python
from functools import partial

import jax
import jax.numpy as jnp
from jax import lax
from jax.experimental import pallas as pl
from jax.experimental.pallas import tpu as pltpu
from jax.sharding import PartitionSpec as P

HD = 72
CLIP = 4
EPS = 1e-06
F32 = jnp.float32
BF16 = jnp.bfloat16


def dot(a, b, ca, cb):
    return lax.dot_general(a, b, (((ca,), (cb,)), ((), ())), preferred_element_type=F32)


def attn_fwd_kernel(scale, qkv_ref, o_ref, p_ref, l_ref, m_ref):
    q, k, v = qkv_ref[0], qkv_ref[1], qkv_ref[2]
    st = dot(k, q, 0, 0) * scale
    peak = jnp.max(st, axis=0, keepdims=True)
    p = jnp.exp(st - peak)
    total = jnp.sum(p, axis=0, keepdims=True)
    pb = p.astype(BF16)
    p_ref[0] = pb
    o_ref[...] = (dot(v, pb, 1, 0) / total).astype(BF16)
    l_ref[0] = total
    m_ref[0] = jnp.broadcast_to(jnp.max(peak, axis=1, keepdims=True), m_ref.shape[1:])


def attn_fwd(qkv, heads):
    _, inner, length = qkv.shape
    return pl.pallas_call(
        partial(attn_fwd_kernel, HD**-0.5),
        grid=(heads,),
        in_specs=[pl.BlockSpec((3, HD, length), lambda h: (0, h, 0))],
        out_specs=[
            pl.BlockSpec((HD, length), lambda h: (h, 0)),
            pl.BlockSpec((1, length, length), lambda h: (h, 0, 0)),
            pl.BlockSpec((1, 1, length), lambda h: (h, 0, 0)),
            pl.BlockSpec((1, 1, 128), lambda h: (h, 0, 0)),
        ],
        out_shape=[
            jax.ShapeDtypeStruct((inner, length), BF16),
            jax.ShapeDtypeStruct((heads, length, length), BF16),
            jax.ShapeDtypeStruct((heads, 1, length), F32),
            jax.ShapeDtypeStruct((heads, 1, 128), F32),
        ],
        cost_estimate=pl.CostEstimate(
            flops=4 * heads * length * length * 256, bytes_accessed=2 * heads * length * length,
            transcendentals=heads * length * length),
        name="attn_fwd",
    )(qkv)


def attn_bwd_kernel(scale, qkv_ref, do_ref, o_ref, p_ref, l_ref, out_ref):
    q, k, v = qkv_ref[0], qkv_ref[1], qkv_ref[2]
    inv = 1.0 / l_ref[0]
    do = do_ref[...].astype(F32)
    dot_row = jnp.sum(do * o_ref[...].astype(F32), axis=0, keepdims=True) * inv
    dos = (do * inv).astype(BF16)
    p = p_ref[0]
    dp = dot(v, dos, 0, 0)
    ds = (p.astype(F32) * (dp - dot_row)).astype(BF16)
    out_ref[2] = dot(dos, p, 1, 1).astype(BF16)
    out_ref[1] = (dot(q, ds, 1, 1) * scale).astype(BF16)
    out_ref[0] = (dot(k, ds, 1, 0) * scale).astype(BF16)


def attn_bwd(qkv, do, o, p, l, heads):
    _, inner, length = qkv.shape
    return pl.pallas_call(
        partial(attn_bwd_kernel, HD**-0.5),
        grid=(heads,),
        in_specs=[
            pl.BlockSpec((3, HD, length), lambda h: (0, h, 0)),
            pl.BlockSpec((HD, length), lambda h: (h, 0)),
            pl.BlockSpec((HD, length), lambda h: (h, 0)),
            pl.BlockSpec((1, length, length), lambda h: (h, 0, 0)),
            pl.BlockSpec((1, 1, length), lambda h: (h, 0, 0)),
        ],
        out_specs=pl.BlockSpec((3, HD, length), lambda h: (0, h, 0)),
        out_shape=jax.ShapeDtypeStruct((3, inner, length), BF16),
        cost_estimate=pl.CostEstimate(
            flops=8 * heads * length * length * 256, bytes_accessed=2 * heads * length * length,
            transcendentals=0),
        name="attn_bwd",
    )(qkv, do, o, p, l)


def norm(rows, gain, shift):
    centre = jnp.mean(rows, axis=1, keepdims=True)
    centred = rows - centre
    inverse = lax.rsqrt(jnp.mean(centred * centred, axis=1, keepdims=True) + EPS)
    normed = centred * inverse
    return normed, inverse, (normed * gain + shift).astype(BF16)


def norm_back(dz, normed, inverse, gain):
    scaled = dz * gain
    first = jnp.mean(scaled, axis=1, keepdims=True)
    second = jnp.mean(scaled * normed, axis=1, keepdims=True)
    return (scaled - first - normed * second) * inverse


def owners_of(slots, parts):
    if slots == 1:
        return [0]
    return [round(j * (parts - 1) / (slots - 1)) for j in range(slots)]


def on_device(
    tokens, slot_valid, ln1_gain, ln1_bias, w_qkv, b_query, b_value, w_out, b_out,
    ln2_gain, ln2_bias, w_up, b_up, w_down, b_down, grad_out,
):
    parts = lax.axis_size("tensor")
    fsdp = lax.axis_size("fsdp")
    me = lax.axis_index("tensor")
    slots, length, width = tokens.shape
    inner_own = b_query.shape[0]
    inner = inner_own * parts
    heads = inner // HD
    units_own = b_up.shape[0]
    rows_own = w_up.shape[0]
    owners = owners_of(slots, parts)
    mine = jnp.int32(0)
    active = jnp.int32(0)
    for j, z in enumerate(owners):
        mine = jnp.where(me == z, j, mine)
        active = jnp.where(me == z, 1, active)

    small = jnp.concatenate(
        [v.astype(F32) for v in (ln1_gain, ln1_bias, b_query, b_value, b_out, ln2_gain, ln2_bias, b_down, b_up)]
    )
    small = lax.all_gather(small, "tensor", axis=0)
    own = width // parts
    pieces = []
    at = 0
    for size in (own, own, inner_own, inner_own, own, own, own, own, units_own):
        pieces.append(small[:, at : at + size].reshape(-1))
        at += size
    gain_one, bias_one, bias_q, bias_v, bias_out, gain_two, bias_two, bias_down, bias_up = pieces

    def spread(block):
        line = lax.all_gather(block, "tensor", axis=1)
        return lax.all_gather(line.reshape(rows_own, -1), "fsdp", axis=0, tiled=True)

    qkv_own = jnp.transpose(w_qkv, (1, 0, 2)).reshape(rows_own, 3 * inner_own)
    attn_own = jnp.concatenate([qkv_own, jnp.transpose(w_out)], axis=1)
    line = lax.all_gather(attn_own, "tensor", axis=0)
    attn_line = jnp.concatenate(
        [line[z, :, c * inner_own : (c + 1) * inner_own] for c in range(4) for z in range(parts)], axis=1
    )
    attn_full = lax.all_gather(attn_line, "fsdp", axis=0, tiled=True)
    ffn_own = jnp.concatenate([w_up, jnp.transpose(w_down)], axis=1)
    line = lax.all_gather(ffn_own, "tensor", axis=0)
    ffn_line = jnp.concatenate(
        [line[z, :, c * units_own : (c + 1) * units_own] for c in range(2) for z in range(parts)], axis=1
    )
    up_full = lax.all_gather(ffn_line[:, : parts * units_own], "fsdp", axis=0, tiled=True)
    down_full = lax.all_gather(ffn_line[:, parts * units_own :], "fsdp", axis=0, tiled=True)
    qkv_full = attn_full[:, : 3 * inner]
    out_full = attn_full[:, 3 * inner :]

    image = lax.dynamic_index_in_dim(tokens, mine, 0, keepdims=False).astype(F32)
    valid = lax.dynamic_index_in_dim(slot_valid, mine, 0, keepdims=False)
    use = (valid > 0) & (active > 0)
    keep = valid.astype(F32)
    error = lax.dynamic_index_in_dim(grad_out, mine, 0, keepdims=False)
    error = jnp.where(use, error, jnp.zeros_like(error))

    normed_one, inverse_one, a_one = norm(image, gain_one, bias_one)
    qkv_bias = jnp.concatenate([bias_q, jnp.zeros_like(bias_q), bias_v])
    qkv = (dot(qkv_full, a_one, 0, 1) + qkv_bias[:, None]).astype(BF16).reshape(3, inner, length)
    heads_t, probs, totals, peaks = attn_fwd(qkv, heads)
    resid = image + dot(heads_t, out_full, 0, 1) + bias_out
    normed_two, inverse_two, a_two = norm(resid, gain_two, bias_two)
    pre = dot(a_two, up_full, 1, 0) + bias_up
    inner_tanh = jnp.tanh(0.7978845608028654 * (pre + 0.044715 * pre * pre * pre))
    act = (0.5 * pre * (1.0 + inner_tanh)).astype(BF16)
    slope = 0.5 * (1.0 + inner_tanh) + 0.5 * pre * (1.0 - inner_tanh * inner_tanh) * (
        0.7978845608028654 * (1.0 + 3 * 0.044715 * pre * pre)
    )
    layer = ((resid + dot(act, down_full, 1, 1) + bias_down) * keep).astype(BF16)
    layer_all = lax.all_gather(layer, "tensor", axis=0)
    layer_out = jnp.stack([layer_all[z] for z in owners])

    g_down = dot(error, act, 0, 0).astype(BF16)
    d_pre = (dot(error, down_full, 1, 0) * slope).astype(BF16)
    g_up = dot(a_two, d_pre, 0, 0).astype(BF16)
    d_two = dot(d_pre, up_full, 1, 1)
    up_err = error.astype(F32)
    d_resid = up_err + norm_back(d_two, normed_two, inverse_two, gain_two)
    d_attn = d_resid.astype(BF16)
    g_out = dot(d_attn, heads_t, 0, 1).astype(BF16)
    d_heads = dot(out_full, d_attn, 0, 1).astype(BF16)
    d_qkv = attn_bwd(qkv, d_heads, heads_t, probs, totals, heads).reshape(3 * inner, length)
    g_qkv = dot(a_one, d_qkv, 0, 1).astype(BF16)
    d_one = dot(d_qkv, qkv_full, 0, 1)
    d_image = d_resid + norm_back(d_one, normed_one, inverse_one, gain_one)
    image_all = lax.all_gather(d_image.astype(BF16), "tensor", axis=0)
    grad_tokens = jnp.stack([image_all[z] for z in owners]).astype(F32)

    def scatter(block):
        return lax.psum_scatter(block, "fsdp", scatter_dimension=0, tiled=True)

    s_up, s_down, s_out, s_qkv = scatter(g_up), scatter(g_down), scatter(g_out), scatter(g_qkv)

    def by_part(block, count, size):
        return jnp.transpose(block.reshape(rows_own, count, parts, size), (2, 0, 1, 3)).reshape(parts, rows_own, count * size)

    z_ffn = lax.psum_scatter(
        jnp.concatenate([by_part(s_up, 1, units_own), by_part(s_down, 1, units_own)], axis=2),
        "tensor", scatter_dimension=0, tiled=False)
    z_attn = lax.psum_scatter(
        jnp.concatenate([by_part(s_qkv, 3, inner_own), by_part(s_out, 1, inner_own)], axis=2),
        "tensor", scatter_dimension=0, tiled=False)
    grad_up = z_ffn[:, :units_own].astype(F32)
    grad_down = jnp.transpose(z_ffn[:, units_own:]).astype(F32)
    grad_qkv = jnp.transpose(z_attn[:, : 3 * inner_own].reshape(rows_own, 3, inner_own), (1, 0, 2)).astype(F32)
    grad_out_w = jnp.transpose(z_attn[:, 3 * inner_own :]).astype(F32)

    d_qkv_f = d_qkv.astype(F32)
    sums = (
        jnp.sum(d_one * normed_one, axis=0),
        jnp.sum(d_one, axis=0),
        jnp.sum(d_two * normed_two, axis=0),
        jnp.sum(d_two, axis=0),
        jnp.sum(d_attn.astype(F32), axis=0),
        jnp.sum(up_err, axis=0),
        jnp.sum(d_qkv_f[:inner], axis=1),
        jnp.sum(d_qkv_f[2 * inner :], axis=1),
        jnp.sum(d_pre.astype(F32), axis=0),
    )
    sizes = [v.shape[0] // parts for v in sums]
    packed = jnp.concatenate([v.reshape(parts, -1) for v in sums], axis=1)
    packed = lax.psum(packed, ("fsdp", "tensor"))
    packed = lax.dynamic_index_in_dim(packed, me, 0, keepdims=False)
    outs = []
    at = 0
    for size in sizes:
        outs.append(packed[at : at + size])
        at += size
    peaks = jnp.where(use, peaks[:, 0, 0], -1e30)
    peaks = lax.pmax(peaks, ("fsdp", "tensor"))
    heads_own = heads // parts
    top = lax.dynamic_slice_in_dim(peaks, me * heads_own, heads_own, 0)
    factor = jnp.repeat(jnp.sqrt(CLIP / jnp.maximum(top, CLIP * 1.0)), HD)
    clipped = w_qkv[:2].astype(F32) * factor
    return (
        layer_out, grad_tokens, outs[0], outs[1], grad_qkv, outs[6], outs[7], grad_out_w, outs[4],
        outs[2], outs[3], grad_up, outs[8], grad_down, outs[5], top, clipped, b_query.astype(F32) * factor,
    )


def solution(mesh):
    placed = (
        P("fsdp", None, None), P("fsdp"), P("tensor"), P("tensor"), P(None, "fsdp", "tensor"), P("tensor"),
        P("tensor"), P("tensor", "fsdp"), P("tensor"), P("tensor"), P("tensor"), P("fsdp", "tensor"),
        P("tensor"), P("tensor", "fsdp"), P("tensor"), P("fsdp", None, None),
    )
    return jax.shard_map(
        on_device,
        mesh=mesh,
        in_specs=placed,
        out_specs=(
            P("fsdp", None, None), P("fsdp", None, None), P("tensor"), P("tensor"), P(None, "fsdp", "tensor"),
            P("tensor"), P("tensor"), P("tensor", "fsdp"), P("tensor"), P("tensor"), P("tensor"),
            P("fsdp", "tensor"), P("tensor"), P("tensor", "fsdp"), P("tensor"), P("tensor"),
            P(None, "fsdp", "tensor"), P("tensor"),
        ),
        check_vma=False,
    )
```

```python
from functools import partial

import jax
import jax.numpy as jnp
from jax import lax
from jax.experimental import pallas as pl
from jax.experimental.pallas import tpu as pltpu
from jax.sharding import PartitionSpec as P

HD = 72
CLIP = 4
EPS = 1e-06
F32 = jnp.float32
BF16 = jnp.bfloat16


def dot(a, b, ca, cb):
    return lax.dot_general(a, b, (((ca,), (cb,)), ((), ())), preferred_element_type=F32)


def attn_fwd_kernel(scale, qkv_ref, o_ref, p_ref, l_ref, m_ref):
    q, k, v = qkv_ref[0], qkv_ref[1], qkv_ref[2]
    st = dot(k, q, 0, 0) * scale
    peak = jnp.max(st, axis=0, keepdims=True)
    p = jnp.exp(st - peak)
    total = jnp.sum(p, axis=0, keepdims=True)
    pb = p.astype(BF16)
    p_ref[0] = pb
    o_ref[...] = (dot(v, pb, 1, 0) / total).astype(BF16)
    l_ref[0] = total
    m_ref[0] = jnp.broadcast_to(jnp.max(peak, axis=1, keepdims=True), m_ref.shape[1:])


def attn_fwd(qkv, heads):
    _, inner, length = qkv.shape
    return pl.pallas_call(
        partial(attn_fwd_kernel, HD**-0.5),
        grid=(heads,),
        in_specs=[pl.BlockSpec((3, HD, length), lambda h: (0, h, 0))],
        out_specs=[
            pl.BlockSpec((HD, length), lambda h: (h, 0)),
            pl.BlockSpec((1, length, length), lambda h: (h, 0, 0)),
            pl.BlockSpec((1, 1, length), lambda h: (h, 0, 0)),
            pl.BlockSpec((1, 1, 128), lambda h: (h, 0, 0)),
        ],
        out_shape=[
            jax.ShapeDtypeStruct((inner, length), BF16),
            jax.ShapeDtypeStruct((heads, length, length), BF16),
            jax.ShapeDtypeStruct((heads, 1, length), F32),
            jax.ShapeDtypeStruct((heads, 1, 128), F32),
        ],
        cost_estimate=pl.CostEstimate(
            flops=4 * heads * length * length * 256, bytes_accessed=2 * heads * length * length,
            transcendentals=heads * length * length),
        name="attn_fwd",
    )(qkv)


def attn_bwd_kernel(scale, qkv_ref, do_ref, o_ref, p_ref, l_ref, out_ref):
    q, k, v = qkv_ref[0], qkv_ref[1], qkv_ref[2]
    inv = 1.0 / l_ref[0]
    do = do_ref[...].astype(F32)
    dot_row = jnp.sum(do * o_ref[...].astype(F32), axis=0, keepdims=True) * inv
    dos = (do * inv).astype(BF16)
    p = p_ref[0]
    dp = dot(v, dos, 0, 0)
    ds = (p.astype(F32) * (dp - dot_row)).astype(BF16)
    out_ref[2] = dot(dos, p, 1, 1).astype(BF16)
    out_ref[1] = (dot(q, ds, 1, 1) * scale).astype(BF16)
    out_ref[0] = (dot(k, ds, 1, 0) * scale).astype(BF16)


def attn_bwd(qkv, do, o, p, l, heads):
    _, inner, length = qkv.shape
    return pl.pallas_call(
        partial(attn_bwd_kernel, HD**-0.5),
        grid=(heads,),
        in_specs=[
            pl.BlockSpec((3, HD, length), lambda h: (0, h, 0)),
            pl.BlockSpec((HD, length), lambda h: (h, 0)),
            pl.BlockSpec((HD, length), lambda h: (h, 0)),
            pl.BlockSpec((1, length, length), lambda h: (h, 0, 0)),
            pl.BlockSpec((1, 1, length), lambda h: (h, 0, 0)),
        ],
        out_specs=pl.BlockSpec((3, HD, length), lambda h: (0, h, 0)),
        out_shape=jax.ShapeDtypeStruct((3, inner, length), BF16),
        cost_estimate=pl.CostEstimate(
            flops=8 * heads * length * length * 256, bytes_accessed=2 * heads * length * length,
            transcendentals=0),
        name="attn_bwd",
    )(qkv, do, o, p, l)


def norm(rows, gain, shift):
    centre = jnp.mean(rows, axis=1, keepdims=True)
    centred = rows - centre
    inverse = lax.rsqrt(jnp.mean(centred * centred, axis=1, keepdims=True) + EPS)
    normed = centred * inverse
    return normed, inverse, (normed * gain + shift).astype(BF16)


def norm_back(dz, normed, inverse, gain):
    scaled = dz * gain
    first = jnp.mean(scaled, axis=1, keepdims=True)
    second = jnp.mean(scaled * normed, axis=1, keepdims=True)
    return (scaled - first - normed * second) * inverse


def owners_of(slots, parts):
    if slots == 1:
        return [0]
    return [round(j * (parts - 1) / (slots - 1)) for j in range(slots)]


def pick(block, index, axis=0):
    return lax.dynamic_index_in_dim(block, index, axis, keepdims=False)


def plus(a, b):
    return (a.astype(F32) + b.astype(F32)).astype(BF16)


def shift(block, by):
    parts = lax.axis_size("tensor")
    return lax.ppermute(block, "tensor", [(z, (z + by) % parts) for z in range(parts)])


def flip(block, bit):
    size = lax.axis_size("fsdp")
    return lax.ppermute(block, "fsdp", [(i, i ^ (1 << bit)) for i in range(size)])


def line_gather(block):
    parts = lax.axis_size("tensor")
    me = lax.axis_index("tensor")
    near = jnp.stack([block] + [shift(block, k) for k in range(1, parts)])
    return [pick(near, lax.rem(me - z + parts, parts)) for z in range(parts)]


def line_scatter(blocks):
    parts = lax.axis_size("tensor")
    me = lax.axis_index("tensor")
    total = pick(blocks, me).astype(F32)
    for k in range(1, parts):
        total = total + shift(pick(blocks, lax.rem(me + k, parts)), k).astype(F32)
    return total


def line_share(block, owners, chunks):
    parts = lax.axis_size("tensor")
    me = lax.axis_index("tensor")
    rows = block.shape[0]
    step = -(-rows // chunks // 16) * 16
    found = []
    for at in range(0, rows, step):
        part = block[at : min(at + step, rows)]
        below, above = [part], [part]
        for s in range(1, parts):
            up = [(z, z + 1) for z in range(parts - 1) if z - s + 1 in owners]
            down = [(z, z - 1) for z in range(1, parts) if z + s - 1 in owners]
            below.append(lax.ppermute(below[-1], "tensor", up) if up else None)
            above.append(lax.ppermute(above[-1], "tensor", down) if down else None)
        outs = []
        for z in owners:
            out = part
            for other in range(parts):
                if other > z:
                    out = jnp.where(me == other, below[other - z], out)
                elif other < z:
                    out = jnp.where(me == other, above[z - other], out)
            outs.append(out)
        found.append(jnp.stack(outs))
    return jnp.concatenate(found, axis=1)


def plane_scatter(block):
    size = lax.axis_size("fsdp")
    me = lax.axis_index("fsdp")
    bits = size.bit_length() - 1
    rows, cols = block.shape[0] // size, block.shape[1]
    block = block.reshape((2,) * bits + (rows, cols))

    def halve(part, bit, axis):
        own = lax.rem(lax.shift_right_logical(me, bit), 2)
        return plus(pick(part, own, axis), flip(pick(part, 1 - own, axis), bit))

    block = halve(block, 0, bits - 1)
    cut = -(-(rows // 2) // 16) * 16
    outs = []
    for lo, hi, order in ((0, cut, list(range(1, bits))), (cut, rows, list(range(bits - 1, 0, -1)))):
        part = lax.slice_in_dim(block, lo, hi, axis=bits - 1)
        left = list(range(bits - 1, 0, -1))
        for bit in order:
            part = halve(part, bit, left.index(bit))
            left.remove(bit)
        outs.append(part)
    return jnp.concatenate(outs, axis=0)


def on_device(
    tokens, slot_valid, ln1_gain, ln1_bias, w_qkv, b_query, b_value, w_out, b_out,
    ln2_gain, ln2_bias, w_up, b_up, w_down, b_down, grad_out,
):
    parts = lax.axis_size("tensor")
    fsdp = lax.axis_size("fsdp")
    me = lax.axis_index("tensor")
    slots, length, width = tokens.shape
    inner_own = b_query.shape[0]
    inner = inner_own * parts
    heads = inner // HD
    units_own = b_up.shape[0]
    rows_own = w_up.shape[0]
    owners = owners_of(slots, parts)
    mine = jnp.int32(0)
    active = jnp.int32(0)
    for j, z in enumerate(owners):
        mine = jnp.where(me == z, j, mine)
        active = jnp.where(me == z, 1, active)

    qkv_own = jnp.transpose(w_qkv, (1, 0, 2)).reshape(rows_own, 3 * inner_own)
    attn_own = jnp.concatenate([qkv_own, jnp.transpose(w_out)], axis=1)
    line = line_gather(attn_own)
    attn_line = jnp.concatenate(
        [line[z][:, c * inner_own : (c + 1) * inner_own] for c in range(4) for z in range(parts)], axis=1
    )
    attn_full = lax.all_gather(attn_line, "fsdp", axis=0, tiled=True)
    ffn_own = jnp.concatenate([w_up, jnp.transpose(w_down)], axis=1)
    line = line_gather(ffn_own)
    ffn_line = jnp.concatenate(
        [line[z][:, c * units_own : (c + 1) * units_own] for c in range(2) for z in range(parts)], axis=1
    )
    up_full = lax.all_gather(ffn_line[:, : parts * units_own], "fsdp", axis=0, tiled=True)
    down_full = lax.all_gather(ffn_line[:, parts * units_own :], "fsdp", axis=0, tiled=True)
    qkv_full = attn_full[:, : 3 * inner]
    out_full = attn_full[:, 3 * inner :]

    small = jnp.concatenate(
        [v.astype(F32) for v in (ln1_gain, ln1_bias, b_query, b_value, b_out, ln2_gain, ln2_bias, b_down, b_up)]
    )
    small = jnp.stack(line_gather(small))
    own = width // parts
    pieces = []
    at = 0
    for size in (own, own, inner_own, inner_own, own, own, own, own, units_own):
        pieces.append(small[:, at : at + size].reshape(-1))
        at += size
    gain_one, bias_one, bias_q, bias_v, bias_out, gain_two, bias_two, bias_down, bias_up = pieces

    image = pick(tokens, mine).astype(F32)
    valid = pick(slot_valid, mine)
    use = (valid > 0) & (active > 0)
    keep = valid.astype(F32)
    error = pick(grad_out, mine)
    error = jnp.where(use, error, jnp.zeros_like(error))

    normed_one, inverse_one, a_one = norm(image, gain_one, bias_one)
    qkv_bias = jnp.concatenate([bias_q, jnp.zeros_like(bias_q), bias_v])
    qkv = (dot(qkv_full, a_one, 0, 1) + qkv_bias[:, None]).astype(BF16).reshape(3, inner, length)
    heads_t, probs, totals, peaks = attn_fwd(qkv, heads)
    resid = image + dot(heads_t, out_full, 0, 1) + bias_out
    normed_two, inverse_two, a_two = norm(resid, gain_two, bias_two)
    pre = dot(a_two, up_full, 1, 0) + bias_up
    inner_tanh = jnp.tanh(0.7978845608028654 * (pre + 0.044715 * pre * pre * pre))
    act = (0.5 * pre * (1.0 + inner_tanh)).astype(BF16)
    slope = 0.5 * (1.0 + inner_tanh) + 0.5 * pre * (1.0 - inner_tanh * inner_tanh) * (
        0.7978845608028654 * (1.0 + 3 * 0.044715 * pre * pre)
    )
    layer = ((resid + dot(act, down_full, 1, 1) + bias_down) * keep).astype(BF16)
    layer_out = line_share(layer, owners, CHUNKS)

    g_down = dot(error, act, 0, 0).astype(BF16)
    d_pre = (dot(error, down_full, 1, 0) * slope).astype(BF16)
    g_up = dot(a_two, d_pre, 0, 0).astype(BF16)
    d_two = dot(d_pre, up_full, 1, 1)
    d_two, g_up, g_down = lax.optimization_barrier((d_two, g_up, g_down))
    up_err = error.astype(F32)
    d_resid = up_err + norm_back(d_two, normed_two, inverse_two, gain_two)
    d_attn = d_resid.astype(BF16)
    g_out = dot(d_attn, heads_t, 0, 1).astype(BF16)
    d_heads = dot(out_full, d_attn, 0, 1).astype(BF16)
    d_qkv = attn_bwd(qkv, d_heads, heads_t, probs, totals, heads).reshape(3 * inner, length)
    g_qkv = dot(a_one, d_qkv, 0, 1).astype(BF16)
    d_one = dot(d_qkv, qkv_full, 0, 1)
    d_image = d_resid + norm_back(d_one, normed_one, inverse_one, gain_one)
    grad_tokens = line_share(d_image.astype(BF16), owners, CHUNKS).astype(F32)

    def by_part(block, count, size):
        return jnp.transpose(block.reshape(rows_own, count, parts, size), (2, 0, 1, 3)).reshape(parts, rows_own, count * size)

    z_down = line_scatter(by_part(scatter(g_down), 1, units_own))
    z_up = line_scatter(by_part(scatter(g_up), 1, units_own))
    z_out = line_scatter(by_part(scatter_late(g_out), 1, inner_own))
    z_qkv = line_scatter(by_part(scatter_late(g_qkv), 3, inner_own))
    grad_down = jnp.transpose(z_down)
    grad_qkv = jnp.transpose(z_qkv.reshape(rows_own, 3, inner_own), (1, 0, 2))
    grad_out_w = jnp.transpose(z_out)

    d_qkv_f = d_qkv.astype(F32)
    sums = (
        jnp.sum(d_one * normed_one, axis=0),
        jnp.sum(d_one, axis=0),
        jnp.sum(d_two * normed_two, axis=0),
        jnp.sum(d_two, axis=0),
        jnp.sum(d_attn.astype(F32), axis=0),
        jnp.sum(up_err, axis=0),
        jnp.sum(d_qkv_f[:inner], axis=1),
        jnp.sum(d_qkv_f[2 * inner :], axis=1),
        jnp.sum(d_pre.astype(F32), axis=0),
    )
    sizes = [v.shape[0] // parts for v in sums]
    packed = line_scatter(jnp.concatenate([v.reshape(parts, -1) for v in sums], axis=1))
    top = jnp.where(use, peaks[:, 0, 0], -1e30)
    for k in range(1, parts):
        top = jnp.maximum(top, shift(jnp.where(use, peaks[:, 0, 0], -1e30), k))
    for bit in range(fsdp.bit_length() - 1):
        packed = packed + flip(packed, bit)
        top = jnp.maximum(top, flip(top, bit))
    outs = []
    at = 0
    for size in sizes:
        outs.append(packed[at : at + size])
        at += size
    heads_own = heads // parts
    top = lax.dynamic_slice_in_dim(top, me * heads_own, heads_own, 0)
    factor = jnp.repeat(jnp.sqrt(CLIP / jnp.maximum(top, CLIP * 1.0)), HD)
    clipped = w_qkv[:2].astype(F32) * factor
    return (
        layer_out, grad_tokens, outs[0], outs[1], grad_qkv, outs[6], outs[7], grad_out_w, outs[4],
        outs[2], outs[3], z_up, outs[8], grad_down, outs[5], top, clipped, b_query.astype(F32) * factor,
    )


def scatter(block):
    return lax.psum_scatter(block, "fsdp", scatter_dimension=0, tiled=True)


scatter_late = plane_scatter
CHUNKS = 2


def solution(mesh):
    placed = (
        P("fsdp", None, None), P("fsdp"), P("tensor"), P("tensor"), P(None, "fsdp", "tensor"), P("tensor"),
        P("tensor"), P("tensor", "fsdp"), P("tensor"), P("tensor"), P("tensor"), P("fsdp", "tensor"),
        P("tensor"), P("tensor", "fsdp"), P("tensor"), P("fsdp", None, None),
    )
    return jax.shard_map(
        on_device,
        mesh=mesh,
        in_specs=placed,
        out_specs=(
            P("fsdp", None, None), P("fsdp", None, None), P("tensor"), P("tensor"), P(None, "fsdp", "tensor"),
            P("tensor"), P("tensor"), P("tensor", "fsdp"), P("tensor"), P("tensor"), P("tensor"),
            P("fsdp", "tensor"), P("tensor"), P("tensor", "fsdp"), P("tensor"), P("tensor"),
            P(None, "fsdp", "tensor"), P("tensor"),
        ),
        check_vma=False,
    )
```

```python
from functools import partial

import jax
import jax.numpy as jnp
from jax import lax
from jax.experimental import pallas as pl
from jax.experimental.pallas import tpu as pltpu
from jax.sharding import PartitionSpec as P

HD = 72
CLIP = 4
EPS = 1e-06
F32 = jnp.float32
BF16 = jnp.bfloat16


def dot(a, b, ca, cb):
    return lax.dot_general(a, b, (((ca,), (cb,)), ((), ())), preferred_element_type=F32)


def attn_fwd_kernel(scale, qkv_ref, o_ref, p_ref, l_ref, m_ref):
    q, k, v = qkv_ref[0], qkv_ref[1], qkv_ref[2]
    st = dot(k, q, 0, 0) * scale
    peak = jnp.max(st, axis=0, keepdims=True)
    p = jnp.exp(st - peak)
    total = jnp.sum(p, axis=0, keepdims=True)
    pb = p.astype(BF16)
    p_ref[0] = pb
    o_ref[...] = (dot(v, pb, 1, 0) / total).astype(BF16)
    l_ref[0] = total
    m_ref[0] = jnp.broadcast_to(jnp.max(peak, axis=1, keepdims=True), m_ref.shape[1:])


def attn_fwd(qkv, heads):
    _, inner, length = qkv.shape
    return pl.pallas_call(
        partial(attn_fwd_kernel, HD**-0.5),
        grid=(heads,),
        in_specs=[pl.BlockSpec((3, HD, length), lambda h: (0, h, 0))],
        out_specs=[
            pl.BlockSpec((HD, length), lambda h: (h, 0)),
            pl.BlockSpec((1, length, length), lambda h: (h, 0, 0)),
            pl.BlockSpec((1, 1, length), lambda h: (h, 0, 0)),
            pl.BlockSpec((1, 1, 128), lambda h: (h, 0, 0)),
        ],
        out_shape=[
            jax.ShapeDtypeStruct((inner, length), BF16),
            jax.ShapeDtypeStruct((heads, length, length), BF16),
            jax.ShapeDtypeStruct((heads, 1, length), F32),
            jax.ShapeDtypeStruct((heads, 1, 128), F32),
        ],
        cost_estimate=pl.CostEstimate(
            flops=4 * heads * length * length * 256, bytes_accessed=2 * heads * length * length,
            transcendentals=heads * length * length),
        name="attn_fwd",
    )(qkv)


def attn_bwd_kernel(scale, qkv_ref, do_ref, o_ref, p_ref, l_ref, out_ref):
    q, k, v = qkv_ref[0], qkv_ref[1], qkv_ref[2]
    inv = 1.0 / l_ref[0]
    do = do_ref[...].astype(F32)
    dot_row = jnp.sum(do * o_ref[...].astype(F32), axis=0, keepdims=True) * inv
    dos = (do * inv).astype(BF16)
    p = p_ref[0]
    dp = dot(v, dos, 0, 0)
    ds = (p.astype(F32) * (dp - dot_row)).astype(BF16)
    out_ref[2] = dot(dos, p, 1, 1).astype(BF16)
    out_ref[1] = (dot(q, ds, 1, 1) * scale).astype(BF16)
    out_ref[0] = (dot(k, ds, 1, 0) * scale).astype(BF16)


def attn_bwd(qkv, do, o, p, l, heads):
    _, inner, length = qkv.shape
    return pl.pallas_call(
        partial(attn_bwd_kernel, HD**-0.5),
        grid=(heads,),
        in_specs=[
            pl.BlockSpec((3, HD, length), lambda h: (0, h, 0)),
            pl.BlockSpec((HD, length), lambda h: (h, 0)),
            pl.BlockSpec((HD, length), lambda h: (h, 0)),
            pl.BlockSpec((1, length, length), lambda h: (h, 0, 0)),
            pl.BlockSpec((1, 1, length), lambda h: (h, 0, 0)),
        ],
        out_specs=pl.BlockSpec((3, HD, length), lambda h: (0, h, 0)),
        out_shape=jax.ShapeDtypeStruct((3, inner, length), BF16),
        cost_estimate=pl.CostEstimate(
            flops=8 * heads * length * length * 256, bytes_accessed=2 * heads * length * length,
            transcendentals=0),
        name="attn_bwd",
    )(qkv, do, o, p, l)


def norm(rows, gain, shift):
    centre = jnp.mean(rows, axis=1, keepdims=True)
    centred = rows - centre
    inverse = lax.rsqrt(jnp.mean(centred * centred, axis=1, keepdims=True) + EPS)
    normed = centred * inverse
    return normed, inverse, (normed * gain + shift).astype(BF16)


def norm_back(dz, normed, inverse, gain):
    scaled = dz * gain
    first = jnp.mean(scaled, axis=1, keepdims=True)
    second = jnp.mean(scaled * normed, axis=1, keepdims=True)
    return (scaled - first - normed * second) * inverse


def owners_of(slots, parts):
    if slots == 1:
        return [0]
    return [round(j * (parts - 1) / (slots - 1)) for j in range(slots)]


def pick(block, index, axis=0):
    return lax.dynamic_index_in_dim(block, index, axis, keepdims=False)


def shift(block, by):
    parts = lax.axis_size("tensor")
    return lax.ppermute(block, "tensor", [(z, (z + by) % parts) for z in range(parts)])


def line_gather(block):
    parts = lax.axis_size("tensor")
    me = lax.axis_index("tensor")
    near = jnp.stack([block] + [shift(block, k) for k in range(1, parts)])
    return [pick(near, lax.rem(me - z + parts, parts)) for z in range(parts)]


def line_share(block, owners):
    parts = lax.axis_size("tensor")
    me = lax.axis_index("tensor")
    far = [block] + [
        lax.ppermute(block, "tensor", [(z, (z + k) % parts) for z in owners]) for k in range(1, parts)]
    outs = []
    for z in owners:
        out = block
        for k in range(1, parts):
            out = jnp.where(me == (z + k) % parts, far[k], out)
        outs.append(out)
    return jnp.stack(outs)


def wgrad_kernel(x_ref, y_ref, out_ref):
    out_ref[...] = dot(x_ref[...], y_ref[...], 0, 0).astype(BF16)


def wgrad(x, y, tile=512):
    length, width = x.shape
    cols = y.shape[1]
    return pl.pallas_call(
        wgrad_kernel,
        grid=(-(-cols // tile),),
        in_specs=[
            pl.BlockSpec((length, width), lambda i: (0, 0)),
            pl.BlockSpec((length, tile), lambda i: (0, i)),
        ],
        out_specs=pl.BlockSpec((width, tile), lambda i: (0, i)),
        out_shape=jax.ShapeDtypeStruct((width, cols), BF16),
        cost_estimate=pl.CostEstimate(
            flops=2 * length * width * cols, bytes_accessed=2 * (length + width) * cols, transcendentals=0),
        name="wgrad",
    )(x, y)


def add_rows(dst, src, rows):
    step = 16 if rows % 16 == 0 else 8

    def body(i, carry):
        at = pl.ds(pl.multiple_of(i * step, step), step)
        dst[at, :] = (dst[at, :].astype(F32) + src[at, :].astype(F32)).astype(BF16)
        return carry

    lax.fori_loop(0, rows // step, body, 0)


def tail_kernel(plan, *refs):
    parts, fsdp, owners, spans, mats, rows, cut, summed = plan
    bits = fsdp.bit_length() - 1
    part_bits = parts.bit_length() - 1
    chips = fsdp // 2
    slots, chunks = len(owners), len(spans)
    refs = list(refs)
    take = lambda n: [refs.pop(0) for _ in range(n)]
    grads = take(mats)
    image, vec = take(2)
    sums = take(mats)
    shared, total = take(2)
    own = take(mats)
    other = take(mats)
    halves = [[take(bits - 1) for _ in range(2)] for _ in range(mats)]
    walk, meet = take(2)
    core_send, core_recv, local_sem, half_send, half_recv, hop_send, hop_recv, vec_send, vec_recv = take(9)
    place = lax.axis_index("fsdp")
    me = lax.axis_index("tensor")

    def moved(index, mask):
        out = index
        for b in range(8):
            if mask >> b & 1:
                out = out + (1 - 2 * ((index // 2**b) % 2)) * 2**b
        return out

    barrier = pltpu.get_barrier_semaphore()
    for b in range(bits):
        pl.semaphore_signal(barrier, inc=1, device_id={"fsdp": moved(place, 1 << b)}, device_id_type=pl.DeviceIdType.MESH)
    for b in range(part_bits):
        pl.semaphore_signal(barrier, inc=1, device_id={"tensor": moved(me, 1 << b)}, device_id_type=pl.DeviceIdType.MESH)
    for m in range(parts):
        near = [z for z in (m - 1, m + 1) if 0 <= z < parts]

        @pl.when(me == m)
        def _():
            for z in near:
                pl.semaphore_signal(barrier, inc=1, device_id={"tensor": me + (z - m)}, device_id_type=pl.DeviceIdType.MESH)
            pl.semaphore_wait(barrier, bits + part_bits + len(near))

    def hop(j, c, side, m):
        lo, hi = spans[c]
        rows_at = pl.ds(lo, hi - lo)
        src = image.at[rows_at] if owners[j] == m else shared.at[j, rows_at]
        return pltpu.make_async_remote_copy(
            src_ref=src, dst_ref=shared.at[j, rows_at], send_sem=hop_send.at[side, j, c],
            recv_sem=hop_recv.at[j, c], device_id={"tensor": me + (2 * side - 1)},
            device_id_type=pl.DeviceIdType.MESH)

    sent = [[] for _ in range(parts)]

    def send_hop(j, c, side, m):
        hop(j, c, side, m).start()
        sent[m].append((j, c, side))

    def arrive(m, first):
        order = sorted((abs(owners[j] - m) * chunks + c, j, c) for j in range(slots) for c in range(chunks) if owners[j] != m)
        for key, j, c in order:
            if (key < 2 * chunks) != first:
                continue
            side = 1 if m > owners[j] else 0
            hop(j, c, 0 if m > 0 else 1, m).wait_recv()
            if 0 <= m + 2 * side - 1 < parts:
                send_hop(j, c, side, m)

    for m in range(parts):
        if m in owners:

            @pl.when(me == m)
            def _():
                for c in range(chunks):
                    for side in (1, 0):
                        if 0 <= m + 2 * side - 1 < parts:
                            send_hop(owners.index(m), c, side, m)

    mine = place % 2
    chip = place - mine
    order = sorted(range(chips), key=lambda r: (-bin(r).count("1"), r))
    cores, locals_ = {}, {}
    for r in order:
        base = moved(chip, 2 * r)
        for i in range(mats):
            cores[r, i] = pltpu.make_async_remote_copy(
                src_ref=grads[i].at[base + 1 - mine], dst_ref=other[i].at[r], send_sem=core_send.at[i, r],
                recv_sem=core_recv.at[i, r], device_id={"fsdp": moved(place, 1)}, device_id_type=pl.DeviceIdType.MESH)
            cores[r, i].start()
            locals_[r, i] = pltpu.make_async_copy(grads[i].at[base + mine], own[i].at[r], local_sem.at[i, r])
            locals_[r, i].start()
    for r in order:
        for i in range(mats):
            cores[r, i].wait_recv()
            locals_[r, i].wait()
            add_rows(own[i].at[r], other[i].at[r], rows)

    ranges = ((0, cut), (cut, rows))
    orders = (list(range(bits - 1)), list(range(bits - 2, -1, -1)))
    left = [list(range(chips)), list(range(chips))]
    flying = []
    for s in range(bits - 1):
        landing = []
        for h in range(2):
            lo, hi = ranges[h]
            b = 1 << orders[h][s]
            stay = [r for r in left[h] if not r & b]
            left[h] = stay
            for k, r in enumerate(stay):
                for i in range(mats):
                    copy = pltpu.make_async_remote_copy(
                        src_ref=own[i].at[r | b, pl.ds(lo, hi - lo)], dst_ref=halves[i][h][s].at[k],
                        send_sem=half_send.at[i, h, s, k], recv_sem=half_recv.at[i, h, s, k],
                        device_id={"fsdp": moved(place, 2 * b)}, device_id_type=pl.DeviceIdType.MESH)
                    copy.start()
                    flying.append(copy)
                    landing.append((copy, own[i].at[r, pl.ds(lo, hi - lo)], halves[i][h][s].at[k], hi - lo))
        if s == 0:
            walk[0] = vec[...]
            partners = [("fsdp", place, b) for b in range(bits)] + [("tensor", me, b) for b in range(part_bits)]
            for k, (axis, index, b) in enumerate(partners):
                copy = pltpu.make_async_remote_copy(
                    src_ref=walk.at[k], dst_ref=meet.at[k], send_sem=vec_send.at[k], recv_sem=vec_recv.at[k],
                    device_id={axis: moved(index, 1 << b)}, device_id_type=pl.DeviceIdType.MESH)
                copy.start()
                flying.append(copy)
                copy.wait_recv()
                walk[k + 1, :summed] = walk[k, :summed] + meet[k, :summed]
                walk[k + 1, summed:] = jnp.maximum(walk[k, summed:], meet[k, summed:])
            total[...] = walk[len(partners)]
        if s == 0:
            for m in range(parts):

                @pl.when(me == m)
                def _():
                    arrive(m, True)

        for copy, dst, src, count in landing:
            copy.wait_recv()
            add_rows(dst, src, count)
    for i in range(mats):
        sums[i][...] = own[i][0]
    for m in range(parts):

        @pl.when(me == m)
        def _():
            arrive(m, False)
            for j, c, side in sent[m]:
                hop(j, c, side, m).wait_send()

    for r in order:
        for i in range(mats):
            cores[r, i].wait_send()
    for copy in flying:
        copy.wait_send()


def tail(grads, image, vec, summed, owners, chunks):
    parts = lax.axis_size("tensor")
    fsdp = lax.axis_size("fsdp")
    bits, part_bits = fsdp.bit_length() - 1, parts.bit_length() - 1
    chips = fsdp // 2
    length, width = image.shape
    rows = grads[0].shape[0] // fsdp
    grads = [g.reshape(fsdp, rows, g.shape[1]) for g in grads]
    cols = [g.shape[2] for g in grads]
    cut = -(-(rows // 2) // 16) * 16
    step = -(-length // chunks // 16) * 16
    spans = tuple((at, min(at + step, length)) for at in range(0, length, step))
    mats, slots, steps = len(grads), len(owners), bits + part_bits
    any_spec = pl.BlockSpec(memory_space=pl.ANY)
    vmem = pl.BlockSpec(memory_space=pltpu.VMEM)
    scratch = [pltpu.VMEM((chips, rows, c), BF16) for c in cols] * 2
    for c in cols:
        for count in (cut, rows - cut):
            scratch += [pltpu.VMEM((chips >> (s + 1), count, c), BF16) for s in range(bits - 1)]
    scratch += [pltpu.VMEM((steps + 1,) + vec.shape, F32), pltpu.VMEM((steps,) + vec.shape, F32)]
    dma = pltpu.SemaphoreType.DMA
    scratch += [
        dma((mats, chips)), dma((mats, chips)), dma((mats, chips)),
        dma((mats, 2, bits - 1, chips // 2)), dma((mats, 2, bits - 1, chips // 2)),
        dma((2, slots, len(spans))), dma((slots, len(spans))), dma((steps,)), dma((steps,)),
    ]
    plan = (parts, fsdp, tuple(owners), spans, mats, rows, cut, summed)
    return pl.pallas_call(
        partial(tail_kernel, plan),
        in_specs=[any_spec] * (mats + 1) + [vmem],
        out_specs=[vmem] * mats + [any_spec, vmem],
        out_shape=[jax.ShapeDtypeStruct((rows, c), BF16) for c in cols]
        + [jax.ShapeDtypeStruct((slots, length, width), BF16), jax.ShapeDtypeStruct(vec.shape, F32)],
        scratch_shapes=scratch,
        compiler_params=pltpu.CompilerParams(collective_id=0, has_side_effects=True),
        cost_estimate=pl.CostEstimate(flops=0, bytes_accessed=250_000_000, transcendentals=0),
        name="tail",
    )(*grads, image, vec)


def line_kernel(parts, mats, rows, *refs):
    own, outs, up, down = (refs[i * mats : (i + 1) * mats] for i in range(4))
    send_sem, recv_sem = refs[4 * mats :]
    me = lax.axis_index("tensor")
    barrier = pltpu.get_barrier_semaphore()
    step = 16 if rows % 16 == 0 else 8

    def copy(i, t, side, m, way=None):
        land = (down, up)[side][i]
        src = own[i] if m == (parts - 1, 0)[side] else land
        return pltpu.make_async_remote_copy(
            src_ref=src.at[t], dst_ref=land.at[t], send_sem=send_sem.at[side, i, t],
            recv_sem=recv_sem.at[side, i, t], device_id={"tensor": me + (way or 2 * side - 1)},
            device_id_type=pl.DeviceIdType.MESH)

    for m in range(parts):
        near = [z for z in (m - 1, m + 1) if 0 <= z < parts]

        @pl.when(me == m)
        def _():
            for z in near:
                pl.semaphore_signal(barrier, inc=1, device_id={"tensor": me + (z - m)}, device_id_type=pl.DeviceIdType.MESH)
            pl.semaphore_wait(barrier, len(near))

    for m in range(parts):

        @pl.when(me == m)
        def _():
            ups = [(1, t) for t in range(parts - 1, m, -1)]
            downs = [(0, t) for t in range(m)]
            turn = []
            for k in range(parts):
                turn += ups[k : k + 1] + downs[k : k + 1]
            for side, t in turn:
                for i in range(mats):
                    if m != (parts - 1, 0)[side]:
                        copy(i, t, side, m).wait_recv()
                        add_rows((down, up)[side][i].at[t], own[i].at[t], rows)
                    copy(i, t, side, m).start()
            for i in range(mats):
                for side in (1, 0):
                    if m != (parts - 1, 0)[side]:
                        copy(i, m, side, m, 1 - 2 * side).wait_recv()

                def body(k, carry):
                    at = pl.ds(pl.multiple_of(k * step, step), step)
                    value = own[i][m, at, :].astype(F32)
                    if m > 0:
                        value = value + up[i][m, at, :].astype(F32)
                    if m < parts - 1:
                        value = value + down[i][m, at, :].astype(F32)
                    outs[i][at, :] = value
                    return carry

                lax.fori_loop(0, rows // step, body, 0)
            for side, t in turn:
                for i in range(mats):
                    copy(i, t, side, m).wait_send()


def line_reduce(blocks):
    parts = lax.axis_size("tensor")
    mats, rows = len(blocks), blocks[0].shape[1]
    vmem = pl.BlockSpec(memory_space=pltpu.VMEM)
    dma = pltpu.SemaphoreType.DMA
    return pl.pallas_call(
        partial(line_kernel, parts, mats, rows),
        in_specs=[vmem] * mats,
        out_specs=[vmem] * mats,
        out_shape=[jax.ShapeDtypeStruct(b.shape[1:], F32) for b in blocks],
        scratch_shapes=[pltpu.VMEM(b.shape, BF16) for b in blocks] * 2 + [dma((2, mats, parts)), dma((2, mats, parts))],
        compiler_params=pltpu.CompilerParams(collective_id=1, has_side_effects=True),
        cost_estimate=pl.CostEstimate(flops=0, bytes_accessed=200_000_000, transcendentals=0),
        name="line_reduce",
    )(*blocks)


def on_device(
    tokens, slot_valid, ln1_gain, ln1_bias, w_qkv, b_query, b_value, w_out, b_out,
    ln2_gain, ln2_bias, w_up, b_up, w_down, b_down, grad_out,
):
    parts = lax.axis_size("tensor")
    fsdp = lax.axis_size("fsdp")
    me = lax.axis_index("tensor")
    slots, length, width = tokens.shape
    inner_own = b_query.shape[0]
    inner = inner_own * parts
    heads = inner // HD
    units_own = b_up.shape[0]
    rows_own = w_up.shape[0]
    owners = owners_of(slots, parts)
    mine = jnp.int32(0)
    active = jnp.int32(0)
    for j, z in enumerate(owners):
        mine = jnp.where(me == z, j, mine)
        active = jnp.where(me == z, 1, active)

    qkv_own = jnp.transpose(w_qkv, (1, 0, 2)).reshape(rows_own, 3 * inner_own)
    attn_own = jnp.concatenate([qkv_own, jnp.transpose(w_out)], axis=1)
    line = line_gather(attn_own)
    attn_line = jnp.concatenate(
        [line[z][:, c * inner_own : (c + 1) * inner_own] for c in range(4) for z in range(parts)], axis=1
    )
    attn_full = lax.all_gather(attn_line, "fsdp", axis=0, tiled=True)
    ffn_own = jnp.concatenate([w_up, jnp.transpose(w_down)], axis=1)
    line = line_gather(ffn_own)
    ffn_line = jnp.concatenate(
        [line[z][:, c * units_own : (c + 1) * units_own] for c in range(2) for z in range(parts)], axis=1
    )
    up_full = lax.all_gather(ffn_line[:, : parts * units_own], "fsdp", axis=0, tiled=True)
    down_full = lax.all_gather(ffn_line[:, parts * units_own :], "fsdp", axis=0, tiled=True)
    qkv_full = attn_full[:, : 3 * inner]
    out_full = attn_full[:, 3 * inner :]

    small = jnp.concatenate(
        [v.astype(F32) for v in (ln1_gain, ln1_bias, b_query, b_value, b_out, ln2_gain, ln2_bias, b_down, b_up)]
    )
    small = jnp.stack(line_gather(small))
    own = width // parts
    pieces = []
    at = 0
    for size in (own, own, inner_own, inner_own, own, own, own, own, units_own):
        pieces.append(small[:, at : at + size].reshape(-1))
        at += size
    gain_one, bias_one, bias_q, bias_v, bias_out, gain_two, bias_two, bias_down, bias_up = pieces

    image = pick(tokens, mine).astype(F32)
    valid = pick(slot_valid, mine)
    use = (valid > 0) & (active > 0)
    keep = valid.astype(F32)
    error = pick(grad_out, mine)
    error = jnp.where(use, error, jnp.zeros_like(error))

    normed_one, inverse_one, a_one = norm(image, gain_one, bias_one)
    qkv_bias = jnp.concatenate([bias_q, jnp.zeros_like(bias_q), bias_v])
    qkv = (dot(qkv_full, a_one, 0, 1) + qkv_bias[:, None]).astype(BF16).reshape(3, inner, length)
    heads_t, probs, totals, peaks = attn_fwd(qkv, heads)
    resid = image + dot(heads_t, out_full, 0, 1) + bias_out
    normed_two, inverse_two, a_two = norm(resid, gain_two, bias_two)
    pre = dot(a_two, up_full, 1, 0) + bias_up
    inner_tanh = jnp.tanh(0.7978845608028654 * (pre + 0.044715 * pre * pre * pre))
    act = (0.5 * pre * (1.0 + inner_tanh)).astype(BF16)
    slope = 0.5 * (1.0 + inner_tanh) + 0.5 * pre * (1.0 - inner_tanh * inner_tanh) * (
        0.7978845608028654 * (1.0 + 3 * 0.044715 * pre * pre)
    )
    layer = ((resid + dot(act, down_full, 1, 1) + bias_down) * keep).astype(BF16)
    layer_out = line_share(layer, owners)

    g_down = wgrad(error, act)
    d_pre = (dot(error, down_full, 1, 0) * slope).astype(BF16)
    g_up = wgrad(a_two, d_pre)
    d_two = dot(d_pre, up_full, 1, 1)
    d_two, g_up, g_down = lax.optimization_barrier((d_two, g_up, g_down))
    up_err = error.astype(F32)
    d_resid = up_err + norm_back(d_two, normed_two, inverse_two, gain_two)
    d_attn = d_resid.astype(BF16)
    g_out = dot(d_attn, heads_t, 0, 1).astype(BF16)
    d_heads = dot(out_full, d_attn, 0, 1).astype(BF16)
    d_qkv = attn_bwd(qkv, d_heads, heads_t, probs, totals, heads).reshape(3 * inner, length)
    g_qkv = dot(a_one, d_qkv, 0, 1).astype(BF16)
    d_one = dot(d_qkv, qkv_full, 0, 1)
    d_image = d_resid + norm_back(d_one, normed_one, inverse_one, gain_one)
    d_image = d_image.astype(BF16)

    d_qkv_f = d_qkv.astype(F32)
    sums = (
        jnp.sum(d_one * normed_one, axis=0),
        jnp.sum(d_one, axis=0),
        jnp.sum(d_two * normed_two, axis=0),
        jnp.sum(d_two, axis=0),
        jnp.sum(d_attn.astype(F32), axis=0),
        jnp.sum(up_err, axis=0),
        jnp.sum(d_qkv_f[:inner], axis=1),
        jnp.sum(d_qkv_f[2 * inner :], axis=1),
        jnp.sum(d_pre.astype(F32), axis=0),
    )
    sizes = [v.shape[0] // parts for v in sums]
    vec = jnp.concatenate([v.reshape(parts, -1) for v in sums], axis=1).reshape(-1)
    count = vec.shape[0]
    summed = -(-count // 1024) * 8
    vec = jnp.pad(vec, (0, summed * 128 - count)).reshape(summed, 128)
    top = jnp.pad(jnp.where(use, peaks[:, 0, 0], -1e30), (0, 1024 - heads)).reshape(8, 128)
    p_qkv, p_out, shared, vec = tail(
        (g_qkv, g_out), d_image, jnp.concatenate([vec, top]), summed, owners, CHUNKS)
    grad_tokens = jnp.stack([jnp.where(me == z, d_image, shared[j]) for j, z in enumerate(owners)]).astype(F32)
    packed = pick(vec[:summed].reshape(-1)[:count].reshape(parts, -1), me)
    top = vec[summed]

    def by_part(block, count, size):
        return jnp.transpose(block.reshape(rows_own, count, parts, size), (2, 0, 1, 3)).reshape(parts, rows_own, count * size)

    z_down, z_up, z_qkv, z_out = line_reduce([
        by_part(scatter(g_down), 1, units_own), by_part(scatter(g_up), 1, units_own),
        by_part(p_qkv, 3, inner_own), by_part(p_out, 1, inner_own)])
    grad_down = jnp.transpose(z_down)
    grad_qkv = jnp.transpose(z_qkv.reshape(rows_own, 3, inner_own), (1, 0, 2))
    grad_out_w = jnp.transpose(z_out)

    outs = []
    at = 0
    for size in sizes:
        outs.append(packed[at : at + size])
        at += size
    heads_own = heads // parts
    top = lax.dynamic_slice_in_dim(top, me * heads_own, heads_own, 0)
    factor = jnp.repeat(jnp.sqrt(CLIP / jnp.maximum(top, CLIP * 1.0)), HD)
    clipped = w_qkv[:2].astype(F32) * factor
    return (
        layer_out, grad_tokens, outs[0], outs[1], grad_qkv, outs[6], outs[7], grad_out_w, outs[4],
        outs[2], outs[3], z_up, outs[8], grad_down, outs[5], top, clipped, b_query.astype(F32) * factor,
    )


def scatter(block):
    return lax.psum_scatter(block, "fsdp", scatter_dimension=0, tiled=True)


CHUNKS = 2


def solution(mesh):
    placed = (
        P("fsdp", None, None), P("fsdp"), P("tensor"), P("tensor"), P(None, "fsdp", "tensor"), P("tensor"),
        P("tensor"), P("tensor", "fsdp"), P("tensor"), P("tensor"), P("tensor"), P("fsdp", "tensor"),
        P("tensor"), P("tensor", "fsdp"), P("tensor"), P("fsdp", None, None),
    )
    return jax.shard_map(
        on_device,
        mesh=mesh,
        in_specs=placed,
        out_specs=(
            P("fsdp", None, None), P("fsdp", None, None), P("tensor"), P("tensor"), P(None, "fsdp", "tensor"),
            P("tensor"), P("tensor"), P("tensor", "fsdp"), P("tensor"), P("tensor"), P("tensor"),
            P("fsdp", "tensor"), P("tensor"), P("tensor", "fsdp"), P("tensor"), P("tensor"),
            P(None, "fsdp", "tensor"), P("tensor"),
        ),
        check_vma=False,
    )
```

```python
from functools import partial

import jax
import jax.numpy as jnp
from jax import lax
from jax.experimental import pallas as pl
from jax.experimental.pallas import tpu as pltpu
from jax.sharding import PartitionSpec as P

HD = 72
CLIP = 4
EPS = 1e-06
F32 = jnp.float32
BF16 = jnp.bfloat16


def dot(a, b, ca, cb):
    return lax.dot_general(a, b, (((ca,), (cb,)), ((), ())), preferred_element_type=F32)


def attn_fwd_kernel(scale, qkv_ref, o_ref, p_ref, l_ref, m_ref):
    q, k, v = qkv_ref[0], qkv_ref[1], qkv_ref[2]
    st = dot(k, q, 0, 0) * scale
    peak = jnp.max(st, axis=0, keepdims=True)
    p = jnp.exp(st - peak)
    total = jnp.sum(p, axis=0, keepdims=True)
    pb = p.astype(BF16)
    p_ref[0] = pb
    o_ref[...] = (dot(v, pb, 1, 0) / total).astype(BF16)
    l_ref[0] = total
    m_ref[0] = jnp.broadcast_to(jnp.max(peak, axis=1, keepdims=True), m_ref.shape[1:])


def attn_fwd(qkv, heads):
    _, inner, length = qkv.shape
    return pl.pallas_call(
        partial(attn_fwd_kernel, HD**-0.5),
        grid=(heads,),
        in_specs=[pl.BlockSpec((3, HD, length), lambda h: (0, h, 0))],
        out_specs=[
            pl.BlockSpec((HD, length), lambda h: (h, 0)),
            pl.BlockSpec((1, length, length), lambda h: (h, 0, 0)),
            pl.BlockSpec((1, 1, length), lambda h: (h, 0, 0)),
            pl.BlockSpec((1, 1, 128), lambda h: (h, 0, 0)),
        ],
        out_shape=[
            jax.ShapeDtypeStruct((inner, length), BF16),
            jax.ShapeDtypeStruct((heads, length, length), BF16),
            jax.ShapeDtypeStruct((heads, 1, length), F32),
            jax.ShapeDtypeStruct((heads, 1, 128), F32),
        ],
        cost_estimate=pl.CostEstimate(
            flops=4 * heads * length * length * 256, bytes_accessed=2 * heads * length * length,
            transcendentals=heads * length * length),
        name="attn_fwd",
    )(qkv)


def attn_bwd_kernel(scale, qkv_ref, do_ref, o_ref, p_ref, l_ref, out_ref):
    q, k, v = qkv_ref[0], qkv_ref[1], qkv_ref[2]
    inv = 1.0 / l_ref[0]
    do = do_ref[...].astype(F32)
    dot_row = jnp.sum(do * o_ref[...].astype(F32), axis=0, keepdims=True) * inv
    dos = (do * inv).astype(BF16)
    p = p_ref[0]
    dp = dot(v, dos, 0, 0)
    ds = (p.astype(F32) * (dp - dot_row)).astype(BF16)
    out_ref[2] = dot(dos, p, 1, 1).astype(BF16)
    out_ref[1] = (dot(q, ds, 1, 1) * scale).astype(BF16)
    out_ref[0] = (dot(k, ds, 1, 0) * scale).astype(BF16)


def attn_bwd(qkv, do, o, p, l, heads):
    _, inner, length = qkv.shape
    return pl.pallas_call(
        partial(attn_bwd_kernel, HD**-0.5),
        grid=(heads,),
        in_specs=[
            pl.BlockSpec((3, HD, length), lambda h: (0, h, 0)),
            pl.BlockSpec((HD, length), lambda h: (h, 0)),
            pl.BlockSpec((HD, length), lambda h: (h, 0)),
            pl.BlockSpec((1, length, length), lambda h: (h, 0, 0)),
            pl.BlockSpec((1, 1, length), lambda h: (h, 0, 0)),
        ],
        out_specs=pl.BlockSpec((3, HD, length), lambda h: (0, h, 0)),
        out_shape=jax.ShapeDtypeStruct((3, inner, length), BF16),
        cost_estimate=pl.CostEstimate(
            flops=8 * heads * length * length * 256, bytes_accessed=2 * heads * length * length,
            transcendentals=0),
        name="attn_bwd",
    )(qkv, do, o, p, l)


def norm(rows, gain, shift):
    centre = jnp.mean(rows, axis=1, keepdims=True)
    centred = rows - centre
    inverse = lax.rsqrt(jnp.mean(centred * centred, axis=1, keepdims=True) + EPS)
    normed = centred * inverse
    return normed, inverse, (normed * gain + shift).astype(BF16)


def norm_back(dz, normed, inverse, gain):
    scaled = dz * gain
    first = jnp.mean(scaled, axis=1, keepdims=True)
    second = jnp.mean(scaled * normed, axis=1, keepdims=True)
    return (scaled - first - normed * second) * inverse


def owners_of(slots, parts):
    if slots == 1:
        return [0]
    return [round(j * (parts - 1) / (slots - 1)) for j in range(slots)]


def pick(block, index, axis=0):
    return lax.dynamic_index_in_dim(block, index, axis, keepdims=False)


def first_hop(block, owners):
    parts = lax.axis_size("tensor")
    up = [(z, z + 1) for z in owners if z + 1 < parts]
    down = [(z, z - 1) for z in owners if z > 0]
    return lax.ppermute(block, "tensor", up), lax.ppermute(block, "tensor", down)


def far_hop(near, distance, owners):
    parts = lax.axis_size("tensor")
    up = [(z + 1, z + distance) for z in owners if z + distance < parts]
    down = [(z - 1, z - distance) for z in owners if z - distance >= 0]
    return (
        lax.ppermute(near[0], "tensor", up) if up else None,
        lax.ppermute(near[1], "tensor", down) if down else None,
    )


def wgrad_kernel(x_ref, y_ref, out_ref):
    out_ref[...] = dot(x_ref[...], y_ref[...], 0, 0).astype(BF16)


def wgrad(x, y, tile=512):
    length, width = x.shape
    cols = y.shape[1]
    return pl.pallas_call(
        wgrad_kernel,
        grid=(-(-cols // tile),),
        in_specs=[
            pl.BlockSpec((length, width), lambda i: (0, 0)),
            pl.BlockSpec((length, tile), lambda i: (0, i)),
        ],
        out_specs=pl.BlockSpec((width, tile), lambda i: (0, i)),
        out_shape=jax.ShapeDtypeStruct((width, cols), BF16),
        cost_estimate=pl.CostEstimate(
            flops=2 * length * width * cols, bytes_accessed=2 * (length + width) * cols, transcendentals=0),
        name="wgrad",
    )(x, y)


def add_rows(dst, src, rows):
    step = 16 if rows % 16 == 0 else 8

    def body(i, carry):
        at = pl.ds(pl.multiple_of(i * step, step), step)
        dst[at, :] = (dst[at, :].astype(F32) + src[at, :].astype(F32)).astype(BF16)
        return carry

    lax.fori_loop(0, rows // step, body, 0)


def tail_kernel(plan, *refs):
    parts, fsdp, owners, spans, mats, rows, cut, summed = plan
    bits = fsdp.bit_length() - 1
    part_bits = parts.bit_length() - 1
    chips = fsdp // 2
    slots, chunks = len(owners), len(spans)
    refs = list(refs)
    take = lambda n: [refs.pop(0) for _ in range(n)]
    grads = take(mats)
    image, vec = take(2)
    sums = take(mats)
    shared, total = take(2)
    own = take(mats)
    other = take(mats)
    halves = [[take(bits - 1) for _ in range(2)] for _ in range(mats)]
    walk, meet = take(2)
    core_send, core_recv, local_sem, half_send, half_recv, hop_send, hop_recv, vec_send, vec_recv = take(9)
    place = lax.axis_index("fsdp")
    me = lax.axis_index("tensor")

    barrier = pltpu.get_barrier_semaphore()
    for b in range(bits):
        pl.semaphore_signal(barrier, inc=1, device_id={"fsdp": moved(place, 1 << b)}, device_id_type=pl.DeviceIdType.MESH)
    for b in range(part_bits):
        pl.semaphore_signal(barrier, inc=1, device_id={"tensor": moved(me, 1 << b)}, device_id_type=pl.DeviceIdType.MESH)
    for m in range(parts):
        near = [z for z in (m - 1, m + 1) if 0 <= z < parts]

        @pl.when(me == m)
        def _():
            for z in near:
                pl.semaphore_signal(barrier, inc=1, device_id={"tensor": me + (z - m)}, device_id_type=pl.DeviceIdType.MESH)
            pl.semaphore_wait(barrier, bits + part_bits + len(near))

    def hop(j, c, side, m):
        lo, hi = spans[c]
        rows_at = pl.ds(lo, hi - lo)
        src = image.at[rows_at] if owners[j] == m else shared.at[j, rows_at]
        return pltpu.make_async_remote_copy(
            src_ref=src, dst_ref=shared.at[j, rows_at], send_sem=hop_send.at[side, j, c],
            recv_sem=hop_recv.at[j, c], device_id={"tensor": me + (2 * side - 1)},
            device_id_type=pl.DeviceIdType.MESH)

    sent = [[] for _ in range(parts)]

    def send_hop(j, c, side, m):
        hop(j, c, side, m).start()
        sent[m].append((j, c, side))

    def arrive(m, reach):
        order = sorted((abs(owners[j] - m), c, j) for j in range(slots) for c in range(chunks) if owners[j] != m)
        for distance, c, j in order:
            if distance not in reach:
                continue
            side = 1 if m > owners[j] else 0
            hop(j, c, 0 if m > 0 else 1, m).wait_recv()
            if 0 <= m + 2 * side - 1 < parts:
                send_hop(j, c, side, m)

    for m in range(parts):
        if m in owners:

            @pl.when(me == m)
            def _():
                for c in range(chunks):
                    for side in (1, 0):
                        if 0 <= m + 2 * side - 1 < parts:
                            send_hop(owners.index(m), c, side, m)

    mine = place % 2
    chip = place - mine
    order = sorted(range(chips), key=lambda r: (-bin(r).count("1"), r))
    cores, locals_ = {}, {}
    for r in order:
        base = moved(chip, 2 * r)
        for i in range(mats):
            cores[r, i] = pltpu.make_async_remote_copy(
                src_ref=grads[i].at[base + 1 - mine], dst_ref=other[i].at[r], send_sem=core_send.at[i, r],
                recv_sem=core_recv.at[i, r], device_id={"fsdp": moved(place, 1)}, device_id_type=pl.DeviceIdType.MESH)
            cores[r, i].start()
            locals_[r, i] = pltpu.make_async_copy(grads[i].at[base + mine], own[i].at[r], local_sem.at[i, r])
            locals_[r, i].start()
    for r in order:
        for i in range(mats):
            cores[r, i].wait_recv()
            locals_[r, i].wait()
            add_rows(own[i].at[r], other[i].at[r], rows)

    ranges = ((0, cut), (cut, rows))
    orders = (list(range(bits - 1)), list(range(bits - 2, -1, -1)))
    left = [list(range(chips)), list(range(chips))]
    flying = []
    for s in range(bits - 1):
        landing = []
        for h in range(2):
            lo, hi = ranges[h]
            b = 1 << orders[h][s]
            stay = [r for r in left[h] if not r & b]
            left[h] = stay
            for k, r in enumerate(stay):
                for i in range(mats):
                    copy = pltpu.make_async_remote_copy(
                        src_ref=own[i].at[r | b, pl.ds(lo, hi - lo)], dst_ref=halves[i][h][s].at[k],
                        send_sem=half_send.at[i, h, s, k], recv_sem=half_recv.at[i, h, s, k],
                        device_id={"fsdp": moved(place, 2 * b)}, device_id_type=pl.DeviceIdType.MESH)
                    copy.start()
                    flying.append(copy)
                    landing.append((copy, own[i].at[r, pl.ds(lo, hi - lo)], halves[i][h][s].at[k], hi - lo))
        for m in range(parts):

            @pl.when(me == m)
            def _():
                arrive(m, (s + 1,))

        if s == 0:
            walk[0] = vec[...]
            partners = [("fsdp", place, b) for b in range(bits)] + [("tensor", me, b) for b in range(part_bits)]
            for k, (axis, index, b) in enumerate(partners):
                copy = pltpu.make_async_remote_copy(
                    src_ref=walk.at[k], dst_ref=meet.at[k], send_sem=vec_send.at[k], recv_sem=vec_recv.at[k],
                    device_id={axis: moved(index, 1 << b)}, device_id_type=pl.DeviceIdType.MESH)
                copy.start()
                flying.append(copy)
                copy.wait_recv()
                walk[k + 1, :summed] = walk[k, :summed] + meet[k, :summed]
                walk[k + 1, summed:] = jnp.maximum(walk[k, summed:], meet[k, summed:])
            total[...] = walk[len(partners)]
        for copy, dst, src, count in landing:
            copy.wait_recv()
            add_rows(dst, src, count)
    for i in range(mats):
        sums[i][...] = own[i][0]
    for m in range(parts):

        @pl.when(me == m)
        def _():
            arrive(m, range(bits, parts))
            for j, c, side in sent[m]:
                hop(j, c, side, m).wait_send()

    for r in order:
        for i in range(mats):
            cores[r, i].wait_send()
    for copy in flying:
        copy.wait_send()


def tail(grads, image, vec, summed, owners, chunks):
    parts = lax.axis_size("tensor")
    fsdp = lax.axis_size("fsdp")
    bits, part_bits = fsdp.bit_length() - 1, parts.bit_length() - 1
    chips = fsdp // 2
    length, width = image.shape
    rows = grads[0].shape[0] // fsdp
    grads = [g.reshape(fsdp, rows, g.shape[1]) for g in grads]
    cols = [g.shape[2] for g in grads]
    cut = -(-(rows // 2) // 16) * 16
    step = -(-length // chunks // 16) * 16
    spans = tuple((at, min(at + step, length)) for at in range(0, length, step))
    mats, slots, steps = len(grads), len(owners), bits + part_bits
    any_spec = pl.BlockSpec(memory_space=pl.ANY)
    vmem = pl.BlockSpec(memory_space=pltpu.VMEM)
    scratch = [pltpu.VMEM((chips, rows, c), BF16) for c in cols] * 2
    for c in cols:
        for count in (cut, rows - cut):
            scratch += [pltpu.VMEM((chips >> (s + 1), count, c), BF16) for s in range(bits - 1)]
    scratch += [pltpu.VMEM((steps + 1,) + vec.shape, F32), pltpu.VMEM((steps,) + vec.shape, F32)]
    dma = pltpu.SemaphoreType.DMA
    scratch += [
        dma((mats, chips)), dma((mats, chips)), dma((mats, chips)),
        dma((mats, 2, bits - 1, chips // 2)), dma((mats, 2, bits - 1, chips // 2)),
        dma((2, slots, len(spans))), dma((slots, len(spans))), dma((steps,)), dma((steps,)),
    ]
    plan = (parts, fsdp, tuple(owners), spans, mats, rows, cut, summed)
    return pl.pallas_call(
        partial(tail_kernel, plan),
        in_specs=[any_spec] * (mats + 1) + [vmem],
        out_specs=[vmem] * mats + [any_spec, vmem],
        out_shape=[jax.ShapeDtypeStruct((rows, c), BF16) for c in cols]
        + [jax.ShapeDtypeStruct((slots, length, width), BF16), jax.ShapeDtypeStruct(vec.shape, F32)],
        scratch_shapes=scratch,
        compiler_params=pltpu.CompilerParams(collective_id=0, has_side_effects=True),
        cost_estimate=pl.CostEstimate(flops=0, bytes_accessed=250_000_000, transcendentals=0),
        name="tail",
    )(*grads, image, vec)


def moved(index, mask):
    out = index
    for b in range(8):
        if mask >> b & 1:
            out = out + (1 - 2 * ((index // 2**b) % 2)) * 2**b
    return out


def front_kernel(plan, *refs):
    parts, fsdp, rows, cut, thirds = plan
    bits = fsdp.bit_length() - 1
    chips = fsdp // 2
    own, (small, down), full, near, lines = refs[:4], refs[4:6], refs[6:8], refs[8:10], refs[10:12]
    hop_send, hop_recv, plane_send, plane_recv, core_recv, own_sem = refs[12:]
    line = (small, near[0], near[1], down)
    place = lax.axis_index("fsdp")
    me = lax.axis_index("tensor")
    barrier = pltpu.get_barrier_semaphore()
    mesh_id = pl.DeviceIdType.MESH
    for b in range(bits):
        pl.semaphore_signal(barrier, inc=1, device_id={"fsdp": moved(place, 1 << b)}, device_id_type=mesh_id)
    for m in range(parts):
        beside = [z for z in (m - 1, m + 1) if 0 <= z < parts]

        @pl.when(me == m)
        def _():
            for z in beside:
                pl.semaphore_signal(barrier, inc=1, device_id={"tensor": me + (z - m)}, device_id_type=mesh_id)
            pl.semaphore_wait(barrier, bits + len(beside))

    def hop(i, z, side, m):
        return pltpu.make_async_remote_copy(
            src_ref=own[i] if z == m else line[i].at[z], dst_ref=line[i].at[z], send_sem=hop_send.at[i, z, side],
            recv_sem=hop_recv.at[i, z], device_id={"tensor": me + (2 * side - 1)}, device_id_type=mesh_id)

    def along(i):
        line[i][me] = own[i][...]
        for m in range(parts):

            @pl.when(me == m)
            def _():
                sides = [side for side in (0, 1) if 0 <= m + 2 * side - 1 < parts]
                for side in sides:
                    hop(i, m, side, m).start()
                for z in sorted((z for z in range(parts) if z != m), key=lambda z: (abs(z - m), z)):
                    side = 1 if m > z else 0
                    hop(i, z, sides[0], m).wait_recv()
                    if side in sides:
                        hop(i, z, side, m).start()

    halves = ((0, cut), (cut, rows))
    orders = (list(range(bits - 1)), list(range(bits - 2, -1, -1)))
    flying = []

    def step_of(h, r):
        return max([-1] + [s for s, b in enumerate(orders[h]) if r >> b & 1])

    def pass_on(i, h, r):
        lo, hi = halves[h]
        at = pl.ds(lo, hi - lo)
        block = moved(place, 2 * r)
        src = lines[i].at[at] if r == 0 else full[i].at[block, at]
        for s in range(step_of(h, r) + 1, bits - 1):
            b = orders[h][s]
            flying.append(pltpu.make_async_remote_copy(
                src_ref=src, dst_ref=full[i].at[block, at], send_sem=plane_send.at[i, h, r, s],
                recv_sem=plane_recv.at[i, h, r ^ (1 << b)], device_id={"fsdp": moved(place, 2 << b)},
                device_id_type=mesh_id))
            flying[-1].start()
        flying.append(pltpu.make_async_remote_copy(
            src_ref=src, dst_ref=full[i].at[block, at], send_sem=plane_send.at[i, h, r, bits - 1],
            recv_sem=core_recv.at[i, h, r], device_id={"fsdp": moved(place, 1)}, device_id_type=mesh_id))
        flying[-1].start()

    def landed(i, h, r, sem, other):
        lo, hi = halves[h]
        at = pl.ds(lo, hi - lo)
        block = full[i].at[moved(place, 2 * r + other), at]
        pltpu.make_async_remote_copy(
            src_ref=block, dst_ref=block, send_sem=plane_send.at[i, h, r, 0], recv_sem=sem.at[i, h, r],
            device_id={"fsdp": moved(place, 1)}, device_id_type=mesh_id).wait_recv()

    def begin(i):
        keep = pltpu.make_async_copy(lines[i], full[i].at[place], own_sem.at[i])
        keep.start()
        for h in range(2):
            pass_on(i, h, 0)
        return keep

    def go_on(i, last):
        for s in range(bits - 1):
            for h in range(2):
                for r in range(1, chips):
                    if step_of(h, r) == s and (s == bits - 2) == last:
                        landed(i, h, r, plane_recv, 0)
                        pass_on(i, h, r)

    along(0)
    along(1)
    for c in range(4):
        for z in range(parts):
            lines[0][:, (c * parts + z) * thirds : (c * parts + z + 1) * thirds] = near[0][z, :, c * thirds : (c + 1) * thirds]
    keeps = [begin(0)]
    along(2)
    go_on(0, False)
    units = near[1].shape[2]
    for z in range(parts):
        lines[1][:, z * units : (z + 1) * units] = near[1][z]
    keeps.append(begin(1))
    along(3)
    go_on(0, True)
    go_on(1, False)
    go_on(1, True)
    for i in range(2):
        keeps[i].wait()
        for h in range(2):
            for r in range(chips):
                landed(i, h, r, core_recv, 1)
    for copy in flying:
        copy.wait_send()
    for m in range(parts):

        @pl.when(me == m)
        def _():
            for i in range(4):
                for z in range(parts):
                    for side in (0, 1):
                        if 0 <= m + 2 * side - 1 < parts and (z == m or (side == 1) == (m > z)):
                            hop(i, z, side, m).wait_send()


def front(small, attn, up, down):
    parts = lax.axis_size("tensor")
    fsdp = lax.axis_size("fsdp")
    bits = fsdp.bit_length() - 1
    rows = up.shape[0]
    cut = -(-(rows // 2) // 16) * 16
    vmem = pl.BlockSpec(memory_space=pltpu.VMEM)
    dma = pltpu.SemaphoreType.DMA
    wide = [parts * attn.shape[1], parts * up.shape[1]]
    return pl.pallas_call(
        partial(front_kernel, (parts, fsdp, rows, cut, attn.shape[1] // 4)),
        in_specs=[vmem] * 4,
        out_specs=[vmem] * 2 + [pl.BlockSpec(memory_space=pl.ANY)] * 2,
        out_shape=[jax.ShapeDtypeStruct((parts,) + small.shape, F32), jax.ShapeDtypeStruct((parts,) + down.shape, BF16)]
        + [jax.ShapeDtypeStruct((fsdp, rows, c), BF16) for c in wide],
        scratch_shapes=[pltpu.VMEM((parts,) + attn.shape, BF16), pltpu.VMEM((parts,) + up.shape, BF16)]
        + [pltpu.VMEM((rows, c), BF16) for c in wide]
        + [dma((4, parts, 2)), dma((4, parts)), dma((2, 2, fsdp // 2, bits)), dma((2, 2, fsdp // 2)),
           dma((2, 2, fsdp // 2)), dma((2,))],
        compiler_params=pltpu.CompilerParams(collective_id=2, has_side_effects=True),
        cost_estimate=pl.CostEstimate(flops=0, bytes_accessed=250_000_000, transcendentals=0),
        name="front",
    )(small, attn, up, down)


def line_kernel(parts, mats, rows, *refs):
    own, outs, up, down = (refs[i * mats : (i + 1) * mats] for i in range(4))
    send_sem, recv_sem = refs[4 * mats :]
    me = lax.axis_index("tensor")
    barrier = pltpu.get_barrier_semaphore()
    step = 16 if rows % 16 == 0 else 8

    def copy(i, t, side, m, way=None):
        land = (down, up)[side][i]
        src = own[i] if m == (parts - 1, 0)[side] else land
        return pltpu.make_async_remote_copy(
            src_ref=src.at[t], dst_ref=land.at[t], send_sem=send_sem.at[side, i, t],
            recv_sem=recv_sem.at[side, i, t], device_id={"tensor": me + (way or 2 * side - 1)},
            device_id_type=pl.DeviceIdType.MESH)

    for m in range(parts):
        near = [z for z in (m - 1, m + 1) if 0 <= z < parts]

        @pl.when(me == m)
        def _():
            for z in near:
                pl.semaphore_signal(barrier, inc=1, device_id={"tensor": me + (z - m)}, device_id_type=pl.DeviceIdType.MESH)
            pl.semaphore_wait(barrier, len(near))

    for m in range(parts):

        @pl.when(me == m)
        def _():
            ups = [(1, t) for t in range(parts - 1, m, -1)]
            downs = [(0, t) for t in range(m)]
            turn = []
            for k in range(parts):
                turn += ups[k : k + 1] + downs[k : k + 1]
            for side, t in turn:
                for i in range(mats):
                    if m != (parts - 1, 0)[side]:
                        copy(i, t, side, m).wait_recv()
                        add_rows((down, up)[side][i].at[t], own[i].at[t], rows)
                    copy(i, t, side, m).start()
            for i in range(mats):
                for side in (1, 0):
                    if m != (parts - 1, 0)[side]:
                        copy(i, m, side, m, 1 - 2 * side).wait_recv()

                def body(k, carry):
                    at = pl.ds(pl.multiple_of(k * step, step), step)
                    value = own[i][m, at, :].astype(F32)
                    if m > 0:
                        value = value + up[i][m, at, :].astype(F32)
                    if m < parts - 1:
                        value = value + down[i][m, at, :].astype(F32)
                    outs[i][at, :] = value
                    return carry

                lax.fori_loop(0, rows // step, body, 0)
            for side, t in turn:
                for i in range(mats):
                    copy(i, t, side, m).wait_send()


def line_reduce(blocks):
    parts = lax.axis_size("tensor")
    mats, rows = len(blocks), blocks[0].shape[1]
    vmem = pl.BlockSpec(memory_space=pltpu.VMEM)
    dma = pltpu.SemaphoreType.DMA
    return pl.pallas_call(
        partial(line_kernel, parts, mats, rows),
        in_specs=[vmem] * mats,
        out_specs=[vmem] * mats,
        out_shape=[jax.ShapeDtypeStruct(b.shape[1:], F32) for b in blocks],
        scratch_shapes=[pltpu.VMEM(b.shape, BF16) for b in blocks] * 2 + [dma((2, mats, parts)), dma((2, mats, parts))],
        compiler_params=pltpu.CompilerParams(collective_id=1, has_side_effects=True),
        cost_estimate=pl.CostEstimate(flops=0, bytes_accessed=200_000_000, transcendentals=0),
        name="line_reduce",
    )(*blocks)


def on_device(
    tokens, slot_valid, ln1_gain, ln1_bias, w_qkv, b_query, b_value, w_out, b_out,
    ln2_gain, ln2_bias, w_up, b_up, w_down, b_down, grad_out,
):
    parts = lax.axis_size("tensor")
    fsdp = lax.axis_size("fsdp")
    me = lax.axis_index("tensor")
    slots, length, width = tokens.shape
    inner_own = b_query.shape[0]
    inner = inner_own * parts
    heads = inner // HD
    units_own = b_up.shape[0]
    rows_own = w_up.shape[0]
    owners = owners_of(slots, parts)
    mine = jnp.int32(0)
    active = jnp.int32(0)
    for j, z in enumerate(owners):
        mine = jnp.where(me == z, j, mine)
        active = jnp.where(me == z, 1, active)

    qkv_own = jnp.transpose(w_qkv, (1, 0, 2)).reshape(rows_own, 3 * inner_own)
    attn_own = jnp.concatenate([qkv_own, jnp.transpose(w_out)], axis=1)
    small = jnp.concatenate(
        [v.astype(F32) for v in (ln1_gain, ln1_bias, b_query, b_value, b_out, ln2_gain, ln2_bias, b_down, b_up)]
    )
    count = small.shape[0]
    tall = -(-count // 1024) * 8
    small = jnp.pad(small, (0, tall * 128 - count)).reshape(tall, 128)
    small, down_line, attn_full, up_full = front(small, attn_own, w_up, jnp.transpose(w_down))
    small = small.reshape(parts, -1)
    attn_full = attn_full.reshape(width, -1)
    up_full = up_full.reshape(width, -1)
    down_line = jnp.concatenate([down_line[z] for z in range(parts)], axis=1)
    down_full = lax.all_gather(down_line, "fsdp", axis=0, tiled=True)
    qkv_full = attn_full[:, : 3 * inner]
    out_full = attn_full[:, 3 * inner :]

    own = width // parts
    pieces = []
    at = 0
    for size in (own, own, inner_own, inner_own, own, own, own, own, units_own):
        pieces.append(small[:, at : at + size].reshape(-1))
        at += size
    gain_one, bias_one, bias_q, bias_v, bias_out, gain_two, bias_two, bias_down, bias_up = pieces

    image = pick(tokens, mine).astype(F32)
    valid = pick(slot_valid, mine)
    use = (valid > 0) & (active > 0)
    keep = valid.astype(F32)
    error = pick(grad_out, mine)
    error = jnp.where(use, error, jnp.zeros_like(error))

    normed_one, inverse_one, a_one = norm(image, gain_one, bias_one)
    qkv_bias = jnp.concatenate([bias_q, jnp.zeros_like(bias_q), bias_v])
    qkv = (dot(qkv_full, a_one, 0, 1) + qkv_bias[:, None]).astype(BF16).reshape(3, inner, length)
    heads_t, probs, totals, peaks = attn_fwd(qkv, heads)
    resid = image + dot(heads_t, out_full, 0, 1) + bias_out
    normed_two, inverse_two, a_two = norm(resid, gain_two, bias_two)
    pre = dot(a_two, up_full, 1, 0) + bias_up
    inner_tanh = jnp.tanh(0.7978845608028654 * (pre + 0.044715 * pre * pre * pre))
    act = (0.5 * pre * (1.0 + inner_tanh)).astype(BF16)
    slope = 0.5 * (1.0 + inner_tanh) + 0.5 * pre * (1.0 - inner_tanh * inner_tanh) * (
        0.7978845608028654 * (1.0 + 3 * 0.044715 * pre * pre)
    )
    g_down = wgrad(error, act)
    s_down = scatter(g_down)
    layer = ((resid + dot(act, down_full, 1, 1) + bias_down) * keep).astype(BF16)
    layer, error = lax.optimization_barrier((layer, error))
    near = first_hop(layer, owners)

    d_pre = (dot(error, down_full, 1, 0) * slope).astype(BF16)
    g_up = wgrad(a_two, d_pre)
    d_two = dot(d_pre, up_full, 1, 1)
    d_two, g_up, g_down = lax.optimization_barrier((d_two, g_up, g_down))
    up_err = error.astype(F32)
    d_resid = up_err + norm_back(d_two, normed_two, inverse_two, gain_two)
    d_attn = d_resid.astype(BF16)
    g_out = dot(d_attn, heads_t, 0, 1).astype(BF16)
    d_heads = dot(out_full, d_attn, 0, 1).astype(BF16)
    d_qkv = attn_bwd(qkv, d_heads, heads_t, probs, totals, heads).reshape(3 * inner, length)
    d_qkv, near, s_down = lax.optimization_barrier((d_qkv, near, s_down))
    hops = [None, near] + [far_hop(near, d, owners) for d in range(2, parts)]
    g_qkv = dot(a_one, d_qkv, 0, 1).astype(BF16)
    d_one = dot(d_qkv, qkv_full, 0, 1)
    d_image = d_resid + norm_back(d_one, normed_one, inverse_one, gain_one)
    d_image = d_image.astype(BF16)

    d_qkv_f = d_qkv.astype(F32)
    sums = (
        jnp.sum(d_one * normed_one, axis=0),
        jnp.sum(d_one, axis=0),
        jnp.sum(d_two * normed_two, axis=0),
        jnp.sum(d_two, axis=0),
        jnp.sum(d_attn.astype(F32), axis=0),
        jnp.sum(up_err, axis=0),
        jnp.sum(d_qkv_f[:inner], axis=1),
        jnp.sum(d_qkv_f[2 * inner :], axis=1),
        jnp.sum(d_pre.astype(F32), axis=0),
    )
    sizes = [v.shape[0] // parts for v in sums]
    vec = jnp.concatenate([v.reshape(parts, -1) for v in sums], axis=1).reshape(-1)
    count = vec.shape[0]
    summed = -(-count // 1024) * 8
    vec = jnp.pad(vec, (0, summed * 128 - count)).reshape(summed, 128)
    top = jnp.pad(jnp.where(use, peaks[:, 0, 0], -1e30), (0, 1024 - heads)).reshape(8, 128)
    def by_part(block, count, size):
        return jnp.transpose(block.reshape(rows_own, count, parts, size), (2, 0, 1, 3)).reshape(parts, rows_own, count * size)

    p_qkv, p_out, shared, vec = tail(
        (g_qkv, g_out), d_image, jnp.concatenate([vec, top]), summed, owners, CHUNKS)
    grad_tokens = jnp.stack([jnp.where(me == z, d_image, shared[j]) for j, z in enumerate(owners)]).astype(F32)
    packed = pick(vec[:summed].reshape(-1)[:count].reshape(parts, -1), me)
    top = vec[summed]

    z_down, z_up, z_qkv, z_out = line_reduce([
        by_part(s_down, 1, units_own), by_part(scatter(g_up), 1, units_own),
        by_part(p_qkv, 3, inner_own), by_part(p_out, 1, inner_own)])
    z_out, hops = lax.optimization_barrier((z_out, hops))
    spread = []
    for z in owners:
        out = layer
        for other in range(parts):
            if other != z:
                out = jnp.where(me == other, hops[abs(other - z)][0 if other > z else 1], out)
        spread.append(out)
    layer_out = jnp.stack(spread)
    grad_down = jnp.transpose(z_down)
    grad_qkv = jnp.transpose(z_qkv.reshape(rows_own, 3, inner_own), (1, 0, 2))
    grad_out_w = jnp.transpose(z_out)

    outs = []
    at = 0
    for size in sizes:
        outs.append(packed[at : at + size])
        at += size
    heads_own = heads // parts
    top = lax.dynamic_slice_in_dim(top, me * heads_own, heads_own, 0)
    factor = jnp.repeat(jnp.sqrt(CLIP / jnp.maximum(top, CLIP * 1.0)), HD)
    clipped = w_qkv[:2].astype(F32) * factor
    return (
        layer_out, grad_tokens, outs[0], outs[1], grad_qkv, outs[6], outs[7], grad_out_w, outs[4],
        outs[2], outs[3], z_up, outs[8], grad_down, outs[5], top, clipped, b_query.astype(F32) * factor,
    )


def scatter(block):
    return lax.psum_scatter(block, "fsdp", scatter_dimension=0, tiled=True)


CHUNKS = 3


def solution(mesh):
    placed = (
        P("fsdp", None, None), P("fsdp"), P("tensor"), P("tensor"), P(None, "fsdp", "tensor"), P("tensor"),
        P("tensor"), P("tensor", "fsdp"), P("tensor"), P("tensor"), P("tensor"), P("fsdp", "tensor"),
        P("tensor"), P("tensor", "fsdp"), P("tensor"), P("fsdp", None, None),
    )
    return jax.shard_map(
        on_device,
        mesh=mesh,
        in_specs=placed,
        out_specs=(
            P("fsdp", None, None), P("fsdp", None, None), P("tensor"), P("tensor"), P(None, "fsdp", "tensor"),
            P("tensor"), P("tensor"), P("tensor", "fsdp"), P("tensor"), P("tensor"), P("tensor"),
            P("fsdp", "tensor"), P("tensor"), P("tensor", "fsdp"), P("tensor"), P("tensor"),
            P(None, "fsdp", "tensor"), P("tensor"),
        ),
        check_vma=False,
    )
```

```python
from functools import partial

import jax
import jax.numpy as jnp
from jax import lax
from jax.experimental import pallas as pl
from jax.experimental.pallas import tpu as pltpu
from jax.sharding import PartitionSpec as P

HD = 72
CLIP = 4
EPS = 1e-06
F32 = jnp.float32
BF16 = jnp.bfloat16


def dot(a, b, ca, cb):
    return lax.dot_general(a, b, (((ca,), (cb,)), ((), ())), preferred_element_type=F32)


def attn_fwd_kernel(scale, qkv_ref, o_ref, p_ref, l_ref, m_ref):
    q, k, v = qkv_ref[0], qkv_ref[1], qkv_ref[2]
    st = dot(k, q, 0, 0) * scale
    peak = jnp.max(st, axis=0, keepdims=True)
    p = jnp.exp(st - peak)
    total = jnp.sum(p, axis=0, keepdims=True)
    pb = p.astype(BF16)
    p_ref[0] = pb
    o_ref[...] = (dot(v, pb, 1, 0) / total).astype(BF16)
    l_ref[0] = total
    m_ref[0] = jnp.broadcast_to(jnp.max(peak, axis=1, keepdims=True), m_ref.shape[1:])


def attn_fwd(qkv, heads):
    _, inner, length = qkv.shape
    return pl.pallas_call(
        partial(attn_fwd_kernel, HD**-0.5),
        grid=(heads,),
        in_specs=[pl.BlockSpec((3, HD, length), lambda h: (0, h, 0))],
        out_specs=[
            pl.BlockSpec((HD, length), lambda h: (h, 0)),
            pl.BlockSpec((1, length, length), lambda h: (h, 0, 0)),
            pl.BlockSpec((1, 1, length), lambda h: (h, 0, 0)),
            pl.BlockSpec((1, 1, 128), lambda h: (h, 0, 0)),
        ],
        out_shape=[
            jax.ShapeDtypeStruct((inner, length), BF16),
            jax.ShapeDtypeStruct((heads, length, length), BF16),
            jax.ShapeDtypeStruct((heads, 1, length), F32),
            jax.ShapeDtypeStruct((heads, 1, 128), F32),
        ],
        cost_estimate=pl.CostEstimate(
            flops=4 * heads * length * length * 256, bytes_accessed=2 * heads * length * length,
            transcendentals=heads * length * length),
        name="attn_fwd",
    )(qkv)


def attn_bwd_kernel(scale, qkv_ref, do_ref, o_ref, p_ref, l_ref, out_ref):
    q, k, v = qkv_ref[0], qkv_ref[1], qkv_ref[2]
    inv = 1.0 / l_ref[0]
    do = do_ref[...].astype(F32)
    dot_row = jnp.sum(do * o_ref[...].astype(F32), axis=0, keepdims=True) * inv
    dos = (do * inv).astype(BF16)
    p = p_ref[0]
    dp = dot(v, dos, 0, 0)
    ds = (p.astype(F32) * (dp - dot_row)).astype(BF16)
    out_ref[2] = dot(dos, p, 1, 1).astype(BF16)
    out_ref[1] = (dot(q, ds, 1, 1) * scale).astype(BF16)
    out_ref[0] = (dot(k, ds, 1, 0) * scale).astype(BF16)


def attn_bwd(qkv, do, o, p, l, heads):
    _, inner, length = qkv.shape
    return pl.pallas_call(
        partial(attn_bwd_kernel, HD**-0.5),
        grid=(heads,),
        in_specs=[
            pl.BlockSpec((3, HD, length), lambda h: (0, h, 0)),
            pl.BlockSpec((HD, length), lambda h: (h, 0)),
            pl.BlockSpec((HD, length), lambda h: (h, 0)),
            pl.BlockSpec((1, length, length), lambda h: (h, 0, 0)),
            pl.BlockSpec((1, 1, length), lambda h: (h, 0, 0)),
        ],
        out_specs=pl.BlockSpec((3, HD, length), lambda h: (0, h, 0)),
        out_shape=jax.ShapeDtypeStruct((3, inner, length), BF16),
        cost_estimate=pl.CostEstimate(
            flops=8 * heads * length * length * 256, bytes_accessed=2 * heads * length * length,
            transcendentals=0),
        name="attn_bwd",
    )(qkv, do, o, p, l)


def project_kernel(w_ref, a_ref, bias_ref, out_ref):
    out_ref[...] = (dot(w_ref[...], a_ref[...], 0, 1) + bias_ref[...]).astype(BF16)


def project(w, a, bias, tile=384):
    length, width = a.shape
    count = bias.shape[0]
    return pl.pallas_call(
        project_kernel,
        grid=(-(-count // tile),),
        in_specs=[
            pl.BlockSpec((width, tile), lambda i: (0, i)),
            pl.BlockSpec((length, width), lambda i: (0, 0)),
            pl.BlockSpec((tile, 1), lambda i: (i, 0)),
        ],
        out_specs=pl.BlockSpec((tile, length), lambda i: (i, 0)),
        out_shape=jax.ShapeDtypeStruct((count, length), BF16),
        cost_estimate=pl.CostEstimate(
            flops=2 * length * width * count, bytes_accessed=2 * (length + width) * count, transcendentals=0),
        name="project",
    )(w, a, bias[:, None])


def norm(rows, gain, shift):
    centre = jnp.mean(rows, axis=1, keepdims=True)
    centred = rows - centre
    inverse = lax.rsqrt(jnp.mean(centred * centred, axis=1, keepdims=True) + EPS)
    normed = centred * inverse
    return normed, inverse, (normed * gain + shift).astype(BF16)


def norm_back(dz, normed, inverse, gain):
    scaled = dz * gain
    first = jnp.mean(scaled, axis=1, keepdims=True)
    second = jnp.mean(scaled * normed, axis=1, keepdims=True)
    return (scaled - first - normed * second) * inverse


def owners_of(slots, parts):
    if slots == 1:
        return [0]
    return [round(j * (parts - 1) / (slots - 1)) for j in range(slots)]


def pick(block, index, axis=0):
    return lax.dynamic_index_in_dim(block, index, axis, keepdims=False)


def first_hop(block, owners):
    parts = lax.axis_size("tensor")
    up = [(z, z + 1) for z in owners if z + 1 < parts]
    down = [(z, z - 1) for z in owners if z > 0]
    return lax.ppermute(block, "tensor", up), lax.ppermute(block, "tensor", down)


def far_hop(near, distance, owners):
    parts = lax.axis_size("tensor")
    up = [(z + 1, z + distance) for z in owners if z + distance < parts]
    down = [(z - 1, z - distance) for z in owners if z - distance >= 0]
    return (
        lax.ppermute(near[0], "tensor", up) if up else None,
        lax.ppermute(near[1], "tensor", down) if down else None,
    )


def wgrad_kernel(x_ref, y_ref, out_ref):
    out_ref[...] = dot(x_ref[...], y_ref[...], 0, 0).astype(BF16)


def wgrad(x, y, tile=512):
    length, width = x.shape
    cols = y.shape[1]
    return pl.pallas_call(
        wgrad_kernel,
        grid=(-(-cols // tile),),
        in_specs=[
            pl.BlockSpec((length, width), lambda i: (0, 0)),
            pl.BlockSpec((length, tile), lambda i: (0, i)),
        ],
        out_specs=pl.BlockSpec((width, tile), lambda i: (0, i)),
        out_shape=jax.ShapeDtypeStruct((width, cols), BF16),
        cost_estimate=pl.CostEstimate(
            flops=2 * length * width * cols, bytes_accessed=2 * (length + width) * cols, transcendentals=0),
        name="wgrad",
    )(x, y)


def add_rows(dst, src, rows):
    step = 16 if rows % 16 == 0 else 8

    def body(i, carry):
        at = pl.ds(pl.multiple_of(i * step, step), step)
        dst[at, :] = (dst[at, :].astype(F32) + src[at, :].astype(F32)).astype(BF16)
        return carry

    lax.fori_loop(0, rows // step, body, 0)


def tail_kernel(plan, *refs):
    parts, fsdp, owners, spans, mats, rows, cut, summed = plan
    bits = fsdp.bit_length() - 1
    part_bits = parts.bit_length() - 1
    chips = fsdp // 2
    slots, chunks = len(owners), len(spans)
    refs = list(refs)
    take = lambda n: [refs.pop(0) for _ in range(n)]
    grads = take(mats)
    image, vec = take(2)
    sums = take(mats)
    shared, total = take(2)
    own = take(mats)
    other = take(mats)
    halves = [[take(bits - 1) for _ in range(2)] for _ in range(mats)]
    walk, meet = take(2)
    core_send, core_recv, local_sem, half_send, half_recv, hop_send, hop_recv, vec_send, vec_recv = take(9)
    place = lax.axis_index("fsdp")
    me = lax.axis_index("tensor")

    barrier = pltpu.get_barrier_semaphore()
    for b in range(bits):
        pl.semaphore_signal(barrier, inc=1, device_id={"fsdp": moved(place, 1 << b)}, device_id_type=pl.DeviceIdType.MESH)
    for b in range(part_bits):
        pl.semaphore_signal(barrier, inc=1, device_id={"tensor": moved(me, 1 << b)}, device_id_type=pl.DeviceIdType.MESH)
    for m in range(parts):
        near = [z for z in (m - 1, m + 1) if 0 <= z < parts]

        @pl.when(me == m)
        def _():
            for z in near:
                pl.semaphore_signal(barrier, inc=1, device_id={"tensor": me + (z - m)}, device_id_type=pl.DeviceIdType.MESH)
            pl.semaphore_wait(barrier, bits + part_bits + len(near))

    def hop(j, c, side, m):
        lo, hi = spans[c]
        rows_at = pl.ds(lo, hi - lo)
        src = image.at[rows_at] if owners[j] == m else shared.at[j, rows_at]
        return pltpu.make_async_remote_copy(
            src_ref=src, dst_ref=shared.at[j, rows_at], send_sem=hop_send.at[side, j, c],
            recv_sem=hop_recv.at[j, c], device_id={"tensor": me + (2 * side - 1)},
            device_id_type=pl.DeviceIdType.MESH)

    sent = [[] for _ in range(parts)]

    def send_hop(j, c, side, m):
        hop(j, c, side, m).start()
        sent[m].append((j, c, side))

    def arrive(m, reach):
        order = sorted((abs(owners[j] - m), c, j) for j in range(slots) for c in range(chunks) if owners[j] != m)
        for distance, c, j in order:
            if distance not in reach:
                continue
            side = 1 if m > owners[j] else 0
            hop(j, c, 0 if m > 0 else 1, m).wait_recv()
            if 0 <= m + 2 * side - 1 < parts:
                send_hop(j, c, side, m)

    for m in range(parts):
        if m in owners:

            @pl.when(me == m)
            def _():
                for c in range(chunks):
                    for side in (1, 0):
                        if 0 <= m + 2 * side - 1 < parts:
                            send_hop(owners.index(m), c, side, m)

    mine = place % 2
    chip = place - mine
    order = sorted(range(chips), key=lambda r: (-bin(r).count("1"), r))
    cores, locals_ = {}, {}
    for r in order:
        base = moved(chip, 2 * r)
        for i in range(mats):
            cores[r, i] = pltpu.make_async_remote_copy(
                src_ref=grads[i].at[base + 1 - mine], dst_ref=other[i].at[r], send_sem=core_send.at[i, r],
                recv_sem=core_recv.at[i, r], device_id={"fsdp": moved(place, 1)}, device_id_type=pl.DeviceIdType.MESH)
            cores[r, i].start()
            locals_[r, i] = pltpu.make_async_copy(grads[i].at[base + mine], own[i].at[r], local_sem.at[i, r])
            locals_[r, i].start()
    for r in order:
        for i in range(mats):
            cores[r, i].wait_recv()
            locals_[r, i].wait()
            add_rows(own[i].at[r], other[i].at[r], rows)

    ranges = ((0, cut), (cut, rows))
    orders = (list(range(bits - 1)), list(range(bits - 2, -1, -1)))
    left = [list(range(chips)), list(range(chips))]
    flying = []
    for s in range(bits - 1):
        landing = []
        for h in range(2):
            lo, hi = ranges[h]
            b = 1 << orders[h][s]
            stay = [r for r in left[h] if not r & b]
            left[h] = stay
            for k, r in enumerate(stay):
                for i in range(mats):
                    copy = pltpu.make_async_remote_copy(
                        src_ref=own[i].at[r | b, pl.ds(lo, hi - lo)], dst_ref=halves[i][h][s].at[k],
                        send_sem=half_send.at[i, h, s, k], recv_sem=half_recv.at[i, h, s, k],
                        device_id={"fsdp": moved(place, 2 * b)}, device_id_type=pl.DeviceIdType.MESH)
                    copy.start()
                    flying.append(copy)
                    landing.append((copy, own[i].at[r, pl.ds(lo, hi - lo)], halves[i][h][s].at[k], hi - lo))
        for m in range(parts):

            @pl.when(me == m)
            def _():
                arrive(m, (s + 1,))

        if s == 0:
            walk[0] = vec[...]
            partners = [("fsdp", place, b) for b in range(bits)] + [("tensor", me, b) for b in range(part_bits)]
            for k, (axis, index, b) in enumerate(partners):
                copy = pltpu.make_async_remote_copy(
                    src_ref=walk.at[k], dst_ref=meet.at[k], send_sem=vec_send.at[k], recv_sem=vec_recv.at[k],
                    device_id={axis: moved(index, 1 << b)}, device_id_type=pl.DeviceIdType.MESH)
                copy.start()
                flying.append(copy)
                copy.wait_recv()
                walk[k + 1, :summed] = walk[k, :summed] + meet[k, :summed]
                walk[k + 1, summed:] = jnp.maximum(walk[k, summed:], meet[k, summed:])
            total[...] = walk[len(partners)]
        for copy, dst, src, count in landing:
            copy.wait_recv()
            add_rows(dst, src, count)
    for i in range(mats):
        sums[i][...] = own[i][0]
    for m in range(parts):

        @pl.when(me == m)
        def _():
            arrive(m, range(bits, parts))
            for j, c, side in sent[m]:
                hop(j, c, side, m).wait_send()

    for r in order:
        for i in range(mats):
            cores[r, i].wait_send()
    for copy in flying:
        copy.wait_send()


def tail(grads, image, vec, summed, owners, chunks):
    parts = lax.axis_size("tensor")
    fsdp = lax.axis_size("fsdp")
    bits, part_bits = fsdp.bit_length() - 1, parts.bit_length() - 1
    chips = fsdp // 2
    length, width = image.shape
    rows = grads[0].shape[0] // fsdp
    grads = [g.reshape(fsdp, rows, g.shape[1]) for g in grads]
    cols = [g.shape[2] for g in grads]
    cut = -(-(rows // 2) // 16) * 16
    step = -(-length // chunks // 16) * 16
    spans = tuple((at, min(at + step, length)) for at in range(0, length, step))
    mats, slots, steps = len(grads), len(owners), bits + part_bits
    any_spec = pl.BlockSpec(memory_space=pl.ANY)
    vmem = pl.BlockSpec(memory_space=pltpu.VMEM)
    scratch = [pltpu.VMEM((chips, rows, c), BF16) for c in cols] * 2
    for c in cols:
        for count in (cut, rows - cut):
            scratch += [pltpu.VMEM((chips >> (s + 1), count, c), BF16) for s in range(bits - 1)]
    scratch += [pltpu.VMEM((steps + 1,) + vec.shape, F32), pltpu.VMEM((steps,) + vec.shape, F32)]
    dma = pltpu.SemaphoreType.DMA
    scratch += [
        dma((mats, chips)), dma((mats, chips)), dma((mats, chips)),
        dma((mats, 2, bits - 1, chips // 2)), dma((mats, 2, bits - 1, chips // 2)),
        dma((2, slots, len(spans))), dma((slots, len(spans))), dma((steps,)), dma((steps,)),
    ]
    plan = (parts, fsdp, tuple(owners), spans, mats, rows, cut, summed)
    return pl.pallas_call(
        partial(tail_kernel, plan),
        in_specs=[any_spec] * (mats + 1) + [vmem],
        out_specs=[vmem] * mats + [any_spec, vmem],
        out_shape=[jax.ShapeDtypeStruct((rows, c), BF16) for c in cols]
        + [jax.ShapeDtypeStruct((slots, length, width), BF16), jax.ShapeDtypeStruct(vec.shape, F32)],
        scratch_shapes=scratch,
        compiler_params=pltpu.CompilerParams(collective_id=0, has_side_effects=True),
        cost_estimate=pl.CostEstimate(flops=0, bytes_accessed=250_000_000, transcendentals=0),
        name="tail",
    )(*grads, image, vec)


def moved(index, mask):
    out = index
    for b in range(8):
        if mask >> b & 1:
            out = out + (1 - 2 * ((index // 2**b) % 2)) * 2**b
    return out


def front_kernel(plan, *refs):
    parts, fsdp, rows, cut, thirds = plan
    bits = fsdp.bit_length() - 1
    chips = fsdp // 2
    own, (small, down), full, near, lines = refs[:4], refs[4:6], refs[6:8], refs[8:10], refs[10:12]
    hop_send, hop_recv, plane_send, plane_recv, core_recv, own_sem = refs[12:]
    line = (small, near[0], near[1], down)
    place = lax.axis_index("fsdp")
    me = lax.axis_index("tensor")
    barrier = pltpu.get_barrier_semaphore()
    mesh_id = pl.DeviceIdType.MESH
    for b in range(bits):
        pl.semaphore_signal(barrier, inc=1, device_id={"fsdp": moved(place, 1 << b)}, device_id_type=mesh_id)
    for m in range(parts):
        beside = [z for z in (m - 1, m + 1) if 0 <= z < parts]

        @pl.when(me == m)
        def _():
            for z in beside:
                pl.semaphore_signal(barrier, inc=1, device_id={"tensor": me + (z - m)}, device_id_type=mesh_id)
            pl.semaphore_wait(barrier, bits + len(beside))

    def hop(i, z, side, m):
        return pltpu.make_async_remote_copy(
            src_ref=own[i] if z == m else line[i].at[z], dst_ref=line[i].at[z], send_sem=hop_send.at[i, z, side],
            recv_sem=hop_recv.at[i, z], device_id={"tensor": me + (2 * side - 1)}, device_id_type=mesh_id)

    def along(i):
        line[i][me] = own[i][...]
        for m in range(parts):

            @pl.when(me == m)
            def _():
                sides = [side for side in (0, 1) if 0 <= m + 2 * side - 1 < parts]
                for side in sides:
                    hop(i, m, side, m).start()
                for z in sorted((z for z in range(parts) if z != m), key=lambda z: (abs(z - m), z)):
                    side = 1 if m > z else 0
                    hop(i, z, sides[0], m).wait_recv()
                    if side in sides:
                        hop(i, z, side, m).start()

    halves = ((0, cut), (cut, rows))
    orders = (list(range(bits - 1)), list(range(bits - 2, -1, -1)))
    flying = []

    def step_of(h, r):
        return max([-1] + [s for s, b in enumerate(orders[h]) if r >> b & 1])

    def pass_on(i, h, r):
        lo, hi = halves[h]
        at = pl.ds(lo, hi - lo)
        block = moved(place, 2 * r)
        src = lines[i].at[at] if r == 0 else full[i].at[block, at]
        for s in range(step_of(h, r) + 1, bits - 1):
            b = orders[h][s]
            flying.append(pltpu.make_async_remote_copy(
                src_ref=src, dst_ref=full[i].at[block, at], send_sem=plane_send.at[i, h, r, s],
                recv_sem=plane_recv.at[i, h, r ^ (1 << b)], device_id={"fsdp": moved(place, 2 << b)},
                device_id_type=mesh_id))
            flying[-1].start()
        flying.append(pltpu.make_async_remote_copy(
            src_ref=src, dst_ref=full[i].at[block, at], send_sem=plane_send.at[i, h, r, bits - 1],
            recv_sem=core_recv.at[i, h, r], device_id={"fsdp": moved(place, 1)}, device_id_type=mesh_id))
        flying[-1].start()

    def landed(i, h, r, sem, other):
        lo, hi = halves[h]
        at = pl.ds(lo, hi - lo)
        block = full[i].at[moved(place, 2 * r + other), at]
        pltpu.make_async_remote_copy(
            src_ref=block, dst_ref=block, send_sem=plane_send.at[i, h, r, 0], recv_sem=sem.at[i, h, r],
            device_id={"fsdp": moved(place, 1)}, device_id_type=mesh_id).wait_recv()

    def begin(i):
        keep = pltpu.make_async_copy(lines[i], full[i].at[place], own_sem.at[i])
        keep.start()
        for h in range(2):
            pass_on(i, h, 0)
        return keep

    def go_on(i, last):
        for s in range(bits - 1):
            for h in range(2):
                for r in range(1, chips):
                    if step_of(h, r) == s and (s == bits - 2) == last:
                        landed(i, h, r, plane_recv, 0)
                        pass_on(i, h, r)

    along(0)
    along(1)
    for c in range(4):
        for z in range(parts):
            lines[0][:, (c * parts + z) * thirds : (c * parts + z + 1) * thirds] = near[0][z, :, c * thirds : (c + 1) * thirds]
    keeps = [begin(0)]
    along(2)
    go_on(0, False)
    units = near[1].shape[2]
    for z in range(parts):
        lines[1][:, z * units : (z + 1) * units] = near[1][z]
    keeps.append(begin(1))
    along(3)
    go_on(0, True)
    go_on(1, False)
    go_on(1, True)
    for i in range(2):
        keeps[i].wait()
        for h in range(2):
            for r in range(chips):
                landed(i, h, r, core_recv, 1)
    for copy in flying:
        copy.wait_send()
    for m in range(parts):

        @pl.when(me == m)
        def _():
            for i in range(4):
                for z in range(parts):
                    for side in (0, 1):
                        if 0 <= m + 2 * side - 1 < parts and (z == m or (side == 1) == (m > z)):
                            hop(i, z, side, m).wait_send()


def front(small, attn, up, down):
    parts = lax.axis_size("tensor")
    fsdp = lax.axis_size("fsdp")
    bits = fsdp.bit_length() - 1
    rows = up.shape[0]
    cut = -(-(rows // 2) // 16) * 16
    vmem = pl.BlockSpec(memory_space=pltpu.VMEM)
    dma = pltpu.SemaphoreType.DMA
    wide = [parts * attn.shape[1], parts * up.shape[1]]
    return pl.pallas_call(
        partial(front_kernel, (parts, fsdp, rows, cut, attn.shape[1] // 4)),
        in_specs=[vmem] * 4,
        out_specs=[vmem] * 2 + [pl.BlockSpec(memory_space=pl.ANY)] * 2,
        out_shape=[jax.ShapeDtypeStruct((parts,) + small.shape, F32), jax.ShapeDtypeStruct((parts,) + down.shape, BF16)]
        + [jax.ShapeDtypeStruct((fsdp, rows, c), BF16) for c in wide],
        scratch_shapes=[pltpu.VMEM((parts,) + attn.shape, BF16), pltpu.VMEM((parts,) + up.shape, BF16)]
        + [pltpu.VMEM((rows, c), BF16) for c in wide]
        + [dma((4, parts, 2)), dma((4, parts)), dma((2, 2, fsdp // 2, bits)), dma((2, 2, fsdp // 2)),
           dma((2, 2, fsdp // 2)), dma((2,))],
        compiler_params=pltpu.CompilerParams(collective_id=2, has_side_effects=True),
        cost_estimate=pl.CostEstimate(flops=0, bytes_accessed=250_000_000, transcendentals=0),
        name="front",
    )(small, attn, up, down)


def line_kernel(parts, mats, rows, *refs):
    own, outs, up, down = (refs[i * mats : (i + 1) * mats] for i in range(4))
    send_sem, recv_sem = refs[4 * mats :]
    me = lax.axis_index("tensor")
    barrier = pltpu.get_barrier_semaphore()
    step = 16 if rows % 16 == 0 else 8

    def copy(i, t, side, m, way=None):
        land = (down, up)[side][i]
        src = own[i] if m == (parts - 1, 0)[side] else land
        return pltpu.make_async_remote_copy(
            src_ref=src.at[t], dst_ref=land.at[t], send_sem=send_sem.at[side, i, t],
            recv_sem=recv_sem.at[side, i, t], device_id={"tensor": me + (way or 2 * side - 1)},
            device_id_type=pl.DeviceIdType.MESH)

    for m in range(parts):
        near = [z for z in (m - 1, m + 1) if 0 <= z < parts]

        @pl.when(me == m)
        def _():
            for z in near:
                pl.semaphore_signal(barrier, inc=1, device_id={"tensor": me + (z - m)}, device_id_type=pl.DeviceIdType.MESH)
            pl.semaphore_wait(barrier, len(near))

    for m in range(parts):

        @pl.when(me == m)
        def _():
            ups = [(1, t) for t in range(parts - 1, m, -1)]
            downs = [(0, t) for t in range(m)]
            turn = []
            for k in range(parts):
                turn += ups[k : k + 1] + downs[k : k + 1]
            for side, t in turn:
                for i in range(mats):
                    if m != (parts - 1, 0)[side]:
                        copy(i, t, side, m).wait_recv()
                        add_rows((down, up)[side][i].at[t], own[i].at[t], rows)
                    copy(i, t, side, m).start()
            for i in range(mats):
                for side in (1, 0):
                    if m != (parts - 1, 0)[side]:
                        copy(i, m, side, m, 1 - 2 * side).wait_recv()

                def body(k, carry):
                    at = pl.ds(pl.multiple_of(k * step, step), step)
                    value = own[i][m, at, :].astype(F32)
                    if m > 0:
                        value = value + up[i][m, at, :].astype(F32)
                    if m < parts - 1:
                        value = value + down[i][m, at, :].astype(F32)
                    outs[i][at, :] = value
                    return carry

                lax.fori_loop(0, rows // step, body, 0)
            for side, t in turn:
                for i in range(mats):
                    copy(i, t, side, m).wait_send()


def line_reduce(blocks):
    parts = lax.axis_size("tensor")
    mats, rows = len(blocks), blocks[0].shape[1]
    vmem = pl.BlockSpec(memory_space=pltpu.VMEM)
    dma = pltpu.SemaphoreType.DMA
    return pl.pallas_call(
        partial(line_kernel, parts, mats, rows),
        in_specs=[vmem] * mats,
        out_specs=[vmem] * mats,
        out_shape=[jax.ShapeDtypeStruct(b.shape[1:], F32) for b in blocks],
        scratch_shapes=[pltpu.VMEM(b.shape, BF16) for b in blocks] * 2 + [dma((2, mats, parts)), dma((2, mats, parts))],
        compiler_params=pltpu.CompilerParams(collective_id=1, has_side_effects=True),
        cost_estimate=pl.CostEstimate(flops=0, bytes_accessed=200_000_000, transcendentals=0),
        name="line_reduce",
    )(*blocks)


def on_device(
    tokens, slot_valid, ln1_gain, ln1_bias, w_qkv, b_query, b_value, w_out, b_out,
    ln2_gain, ln2_bias, w_up, b_up, w_down, b_down, grad_out,
):
    parts = lax.axis_size("tensor")
    fsdp = lax.axis_size("fsdp")
    me = lax.axis_index("tensor")
    slots, length, width = tokens.shape
    inner_own = b_query.shape[0]
    inner = inner_own * parts
    heads = inner // HD
    units_own = b_up.shape[0]
    rows_own = w_up.shape[0]
    owners = owners_of(slots, parts)
    mine = jnp.int32(0)
    active = jnp.int32(0)
    for j, z in enumerate(owners):
        mine = jnp.where(me == z, j, mine)
        active = jnp.where(me == z, 1, active)

    qkv_own = jnp.transpose(w_qkv, (1, 0, 2)).reshape(rows_own, 3 * inner_own)
    attn_own = jnp.concatenate([qkv_own, jnp.transpose(w_out)], axis=1)
    small = jnp.concatenate(
        [v.astype(F32) for v in (ln1_gain, ln1_bias, b_query, b_value, b_out, ln2_gain, ln2_bias, b_down, b_up)]
    )
    count = small.shape[0]
    tall = -(-count // 1024) * 8
    small = jnp.pad(small, (0, tall * 128 - count)).reshape(tall, 128)
    small, down_line, attn_full, up_full = front(small, attn_own, w_up, jnp.transpose(w_down))
    small = small.reshape(parts, -1)
    attn_full = attn_full.reshape(width, -1)
    up_full = up_full.reshape(width, -1)
    down_line = jnp.concatenate([down_line[z] for z in range(parts)], axis=1)
    down_full = lax.all_gather(down_line, "fsdp", axis=0, tiled=True)
    qkv_full = attn_full[:, : 3 * inner]
    out_full = attn_full[:, 3 * inner :]

    own = width // parts
    pieces = []
    at = 0
    for size in (own, own, inner_own, inner_own, own, own, own, own, units_own):
        pieces.append(small[:, at : at + size].reshape(-1))
        at += size
    gain_one, bias_one, bias_q, bias_v, bias_out, gain_two, bias_two, bias_down, bias_up = pieces

    image = pick(tokens, mine).astype(F32)
    valid = pick(slot_valid, mine)
    use = (valid > 0) & (active > 0)
    keep = valid.astype(F32)
    error = pick(grad_out, mine)
    error = jnp.where(use, error, jnp.zeros_like(error))

    normed_one, inverse_one, a_one = norm(image, gain_one, bias_one)
    qkv_bias = jnp.concatenate([bias_q, jnp.zeros_like(bias_q), bias_v])
    qkv = project(attn_full, a_one, qkv_bias).reshape(3, inner, length)
    heads_t, probs, totals, peaks = attn_fwd(qkv, heads)
    resid = image + dot(heads_t, out_full, 0, 1) + bias_out
    normed_two, inverse_two, a_two = norm(resid, gain_two, bias_two)
    pre = dot(a_two, up_full, 1, 0) + bias_up
    inner_tanh = jnp.tanh(0.7978845608028654 * (pre + 0.044715 * pre * pre * pre))
    act = (0.5 * pre * (1.0 + inner_tanh)).astype(BF16)
    slope = 0.5 * (1.0 + inner_tanh) + 0.5 * pre * (1.0 - inner_tanh * inner_tanh) * (
        0.7978845608028654 * (1.0 + 3 * 0.044715 * pre * pre)
    )
    g_down = wgrad(error, act)
    s_down = scatter(g_down)
    layer = ((resid + dot(act, down_full, 1, 1) + bias_down) * keep).astype(BF16)
    layer, error = lax.optimization_barrier((layer, error))
    near = first_hop(layer, owners)

    d_pre = (dot(error, down_full, 1, 0) * slope).astype(BF16)
    g_up = wgrad(a_two, d_pre)
    d_two = dot(d_pre, up_full, 1, 1)
    d_two, g_up, g_down, near = lax.optimization_barrier((d_two, g_up, g_down, near))
    hops = [None, near] + [far_hop(near, d, owners) for d in range(2, parts)]
    up_err = error.astype(F32)
    d_resid = up_err + norm_back(d_two, normed_two, inverse_two, gain_two)
    d_attn = d_resid.astype(BF16)
    g_out = dot(d_attn, heads_t, 0, 1).astype(BF16)
    d_heads = dot(out_full, d_attn, 0, 1).astype(BF16)
    d_qkv = attn_bwd(qkv, d_heads, heads_t, probs, totals, heads).reshape(3 * inner, length)
    d_qkv, s_down = lax.optimization_barrier((d_qkv, s_down))
    g_qkv = dot(a_one, d_qkv, 0, 1).astype(BF16)
    d_one = dot(d_qkv, qkv_full, 0, 1)
    d_image = d_resid + norm_back(d_one, normed_one, inverse_one, gain_one)
    d_image = d_image.astype(BF16)

    d_qkv_f = d_qkv.astype(F32)
    sums = (
        jnp.sum(d_one * normed_one, axis=0),
        jnp.sum(d_one, axis=0),
        jnp.sum(d_two * normed_two, axis=0),
        jnp.sum(d_two, axis=0),
        jnp.sum(d_attn.astype(F32), axis=0),
        jnp.sum(up_err, axis=0),
        jnp.sum(d_qkv_f[:inner], axis=1),
        jnp.sum(d_qkv_f[2 * inner :], axis=1),
        jnp.sum(d_pre.astype(F32), axis=0),
    )
    sizes = [v.shape[0] // parts for v in sums]
    vec = jnp.concatenate([v.reshape(parts, -1) for v in sums], axis=1).reshape(-1)
    count = vec.shape[0]
    summed = -(-count // 1024) * 8
    vec = jnp.pad(vec, (0, summed * 128 - count)).reshape(summed, 128)
    top = jnp.pad(jnp.where(use, peaks[:, 0, 0], -1e30), (0, 1024 - heads)).reshape(8, 128)
    def by_part(block, count, size):
        return jnp.transpose(block.reshape(rows_own, count, parts, size), (2, 0, 1, 3)).reshape(parts, rows_own, count * size)

    p_qkv, p_out, shared, vec = tail(
        (g_qkv, g_out), d_image, jnp.concatenate([vec, top]), summed, owners, CHUNKS)
    grad_tokens = jnp.stack([jnp.where(me == z, d_image, shared[j]) for j, z in enumerate(owners)]).astype(F32)
    packed = pick(vec[:summed].reshape(-1)[:count].reshape(parts, -1), me)
    top = vec[summed]

    z_down, z_up, z_qkv, z_out = line_reduce([
        by_part(s_down, 1, units_own), by_part(scatter(g_up), 1, units_own),
        by_part(p_qkv, 3, inner_own), by_part(p_out, 1, inner_own)])
    z_out, hops = lax.optimization_barrier((z_out, hops))
    spread = []
    for z in owners:
        out = layer
        for other in range(parts):
            if other != z:
                out = jnp.where(me == other, hops[abs(other - z)][0 if other > z else 1], out)
        spread.append(out)
    layer_out = jnp.stack(spread)
    grad_down = jnp.transpose(z_down)
    grad_qkv = jnp.transpose(z_qkv.reshape(rows_own, 3, inner_own), (1, 0, 2))
    grad_out_w = jnp.transpose(z_out)

    outs = []
    at = 0
    for size in sizes:
        outs.append(packed[at : at + size])
        at += size
    heads_own = heads // parts
    top = lax.dynamic_slice_in_dim(top, me * heads_own, heads_own, 0)
    factor = jnp.repeat(jnp.sqrt(CLIP / jnp.maximum(top, CLIP * 1.0)), HD)
    clipped = w_qkv[:2].astype(F32) * factor
    return (
        layer_out, grad_tokens, outs[0], outs[1], grad_qkv, outs[6], outs[7], grad_out_w, outs[4],
        outs[2], outs[3], z_up, outs[8], grad_down, outs[5], top, clipped, b_query.astype(F32) * factor,
    )


def scatter(block):
    return lax.psum_scatter(block, "fsdp", scatter_dimension=0, tiled=True)


CHUNKS = 3


def solution(mesh):
    placed = (
        P("fsdp", None, None), P("fsdp"), P("tensor"), P("tensor"), P(None, "fsdp", "tensor"), P("tensor"),
        P("tensor"), P("tensor", "fsdp"), P("tensor"), P("tensor"), P("tensor"), P("fsdp", "tensor"),
        P("tensor"), P("tensor", "fsdp"), P("tensor"), P("fsdp", None, None),
    )
    return jax.shard_map(
        on_device,
        mesh=mesh,
        in_specs=placed,
        out_specs=(
            P("fsdp", None, None), P("fsdp", None, None), P("tensor"), P("tensor"), P(None, "fsdp", "tensor"),
            P("tensor"), P("tensor"), P("tensor", "fsdp"), P("tensor"), P("tensor"), P("tensor"),
            P("fsdp", "tensor"), P("tensor"), P("tensor", "fsdp"), P("tensor"), P("tensor"),
            P(None, "fsdp", "tensor"), P("tensor"),
        ),
        check_vma=False,
    )
```
